256 devices in a mesh: scan: 8 (over y_hi, x), cross: 32 (over y_lo, z, core).
Axes of the slice: x: 4, y: 4 (y_hi: 2, y_lo: 2; y = y_hi * 2 + y_lo), z: 8, core: 2. Of those that a mesh axis runs over, the one named last changes fastest.
Arguments:
- wafer_state: float32 [128, 512, 384], P('scan', 'cross'), may hold values from 0 to 1, as said below
- layer_heat_coefficients: float32 [256], replicated, may hold values from 0.03 to 0.14
- beam_profile: float32 [512], replicated, may hold values from 0.25 to 1.75
- beam_start: int32 [4], replicated, may hold values from 0 to 127
- beam_steps: int32 [4], replicated, may hold values from 1 to 64
Outputs:
- annealed: float32 [128, 512, 384], P('scan', 'cross')
The draws below stay inside these ranges and needn't reach their ends.
Inputs may be any that keep to these rules, and one draw needn't show every extreme that they name: `wafer_state`: temperatures lie in 0 to 0.6, acid in 0 to 1, protection in 0.5 to 1.
All inputs are finite; a program needn't handle non-finite values.
Results may differ from the reference program's by a relative error of at most 0.00002.
Values sent between devices are 32-bit elements; how exact they have to be, the bound alone decides.
A program may use at most 64 MiB of HBM per device.

```python
import math
import jax
import jax.numpy as jnp

DEV_X = 16
RESIST = 64
STEPS = 4
SUBSTEPS = 2
LAYER_BINS_TOTAL = 256
SWEEP_BINS = 128
TRANSVERSE_BINS = 512
HALF_WIDTH = 8


def draw_wafer_state(key, part):
    random_warmth_seed, random_proton_seed, random_guard_seed = jax.random.split(key, 3)
    warmth_grid = 0.6 * jax.random.uniform(random_warmth_seed, (SWEEP_BINS, TRANSVERSE_BINS, LAYER_BINS_TOTAL), jnp.float32)
    acid_fraction = jax.random.uniform(random_proton_seed, (SWEEP_BINS, TRANSVERSE_BINS, RESIST), jnp.float32)
    protected_fraction = 0.5 + 0.5 * jax.random.uniform(random_guard_seed, (SWEEP_BINS, TRANSVERSE_BINS, RESIST), jnp.float32)
    return jnp.concatenate([warmth_grid, acid_fraction, protected_fraction], axis=-1)


def touch_ends(drawn, stream_key, least, top_value):
    place = [jax.random.randint(jax.random.fold_in(stream_key, axis), (), 0, length) for axis, length in enumerate(drawn.shape)]
    widest = drawn.shape.index(max(drawn.shape))
    neighbour = place[:widest] + [(place[widest] + 1) % drawn.shape[widest]] + place[widest + 1:]
    return drawn.at[tuple(place)].set(least).at[tuple(neighbour)].set(top_value)


def setup_inputs(seed: int = 0) -> dict:
    arg_keys = jax.random.split(jax.random.key(seed), 6)
    wafer_state = draw_wafer_state(jax.random.fold_in(arg_keys[5], 71), 0)
    layer_heat_coefficients = jnp.clip(jnp.exp(jax.random.uniform(arg_keys[1], (LAYER_BINS_TOTAL,), jnp.float32, math.log(0.03), math.log(0.14))), 0.03, 0.14)
    beam_profile = jnp.clip(1.0 + 0.15 * jax.random.normal(arg_keys[2], (TRANSVERSE_BINS,), jnp.float32), 0.25, 1.75)
    beam_start = touch_ends(jax.random.randint(arg_keys[3], (STEPS,), 0, SWEEP_BINS), jax.random.fold_in(arg_keys[3], 1), 0, SWEEP_BINS - 1).astype(jnp.int32)
    beam_steps = touch_ends(jax.random.randint(arg_keys[4], (STEPS,), 1, 4 * DEV_X + 1), jax.random.fold_in(arg_keys[4], 1), 1, 4 * DEV_X).astype(jnp.int32)
    return dict(wafer_state=wafer_state, layer_heat_coefficients=layer_heat_coefficients, beam_profile=beam_profile, beam_start=beam_start, beam_steps=beam_steps)


heat_power = 0.5
absorb_depth = 6.0
barrier_energy = 3.0
frequency_multiplier = 0.6
proton_mobility = 0.15


def lateral_heat_current(values, coeffs):
    middle_v = values[1:-1, 1:-1]
    middle_c = coeffs[1:-1, 1:-1]
    flow_sum = jnp.zeros_like(middle_v)
    for other_v, other_c in ((values[2:, 1:-1], coeffs[2:, 1:-1]), (values[:-2, 1:-1], coeffs[:-2, 1:-1]), (values[1:-1, 2:], coeffs[1:-1, 2:]), (values[1:-1, :-2], coeffs[1:-1, :-2])):
        flow_sum = flow_sum + 0.5 * (middle_c + other_c) * (other_v - middle_v)
    return flow_sum


def lower_heat_current(values, coeffs, below_v, below_c):
    upper_v = jnp.concatenate([values[..., :1], values[..., :-1]], axis=-1)
    upper_c = jnp.concatenate([coeffs[..., :1], coeffs[..., :-1]], axis=-1)
    lower_v = jnp.concatenate([values[..., 1:], below_v], axis=-1)
    lower_c = jnp.concatenate([coeffs[..., 1:], below_c], axis=-1)
    return 0.5 * (coeffs + upper_c) * (upper_v - values) + 0.5 * (coeffs + lower_c) * (lower_v - values)


def substep(heated_extent, protected_fraction, layer_heat_coefficients, profile, xcoord, center, spread):
    vertical_cells = layer_heat_coefficients.shape[0]
    polymer_coating = protected_fraction.shape[-1]
    warmth_grid = heated_extent[..., :vertical_cells]
    acid_ext = heated_extent[..., vertical_cells:]
    local_heat_coupling = layer_heat_coefficients / (1.0 + 0.25 * warmth_grid * warmth_grid)
    midpoint_warmth = warmth_grid[1:-1, 1:-1]
    midpoint_heat_ability = local_heat_coupling[1:-1, 1:-1]
    blank_stack_vector = jnp.zeros_like(midpoint_warmth[..., :1])
    heat_current = lateral_heat_current(warmth_grid, local_heat_coupling) + lower_heat_current(midpoint_warmth, midpoint_heat_ability, blank_stack_vector, blank_stack_vector + layer_heat_coefficients[-1])
    depth_level = jnp.arange(vertical_cells, dtype=jnp.float32)
    absorb = jnp.where(depth_level >= polymer_coating, jnp.exp(-(depth_level - polymer_coating) / absorb_depth), 0.0)
    beam_spot = jnp.exp(-jnp.square((xcoord - center) / spread))
    energy_input = heat_power * beam_spot[:, None, None] * profile[None, :, None] * absorb
    updated_warmth = midpoint_warmth + heat_current + energy_input
    polymer_warmth = warmth_grid[..., :polymer_coating]
    spread_proton_site = proton_mobility * polymer_warmth * polymer_warmth / (1.0 + polymer_warmth * polymer_warmth)
    middle_a = acid_ext[1:-1, 1:-1]
    middle_d = spread_proton_site[1:-1, 1:-1]
    new_acid = middle_a + lateral_heat_current(acid_ext, spread_proton_site) + lower_heat_current(middle_a, middle_d, middle_a[..., -1:], middle_d[..., -1:])
    cleavage_rate = frequency_multiplier * jnp.exp(-barrier_energy / (1.0 + midpoint_warmth[..., :polymer_coating]))
    new_protect = protected_fraction * (1.0 - cleavage_rate * middle_a)
    return jnp.concatenate([updated_warmth, new_acid], axis=-1), new_protect


def reference(wafer_state, layer_heat_coefficients, beam_profile, beam_start, beam_steps):
    hot_depth = LAYER_BINS_TOTAL + RESIST
    xcoord = jnp.arange(SWEEP_BINS, dtype=jnp.float32)
    spread = float(HALF_WIDTH)
    for frame_no in range(STEPS):
        for sub_no in range(SUBSTEPS):
            center = (beam_start[frame_no] + sub_no * beam_steps[frame_no]).astype(jnp.float32)
            hot_part = wafer_state[..., :hot_depth]
            heated_extent = jnp.pad(hot_part, ((1, 1), (0, 0), (0, 0)), mode="wrap")
            heated_extent = jnp.pad(heated_extent, ((0, 0), (1, 1), (0, 0)))
            hot_part, protected_fraction = substep(heated_extent, wafer_state[..., hot_depth:], layer_heat_coefficients, beam_profile, xcoord, center, spread)
            wafer_state = jnp.concatenate([hot_part, protected_fraction], axis=-1)
        wafer_state = jnp.roll(wafer_state, -DEV_X, axis=0)
        wafer_state = wafer_state.at[SWEEP_BINS - DEV_X:, :, :LAYER_BINS_TOTAL].set(0.0)
    return wafer_state
```

```python
import jax
import jax.numpy as jnp
from jax import lax
from jax.experimental import pallas as pl
from jax.experimental.pallas import tpu as pltpu
from jax.sharding import PartitionSpec as P

STEPS = 4
SUBSTEPS = 2
LEVELS = STEPS * SUBSTEPS
HALO = LEVELS
MESH = pl.DeviceIdType.MESH

heat_power = 0.5
absorb_depth = 6.0
barrier_energy = 3.0
frequency_multiplier = 0.6
proton_mobility = 0.15


def lane_roll(v, shift):
    return pltpu.roll(v, shift % v.shape[1], axis=1)


def sub_roll(v, shift):
    return pltpu.roll(v, shift % v.shape[0], axis=0)


def kernel(
    profile_ref, start_ref, steps_ref, coef_ref, x_ref, o_ref,
    st, qb, db, pb, spot, pa, send_sems, recv_sems, own_sem, out_sems, got_sems,
):
    s = lax.axis_index("scan")
    c = lax.axis_index("cross")
    n_scan = lax.axis_size("scan")
    n_cross = lax.axis_size("cross")
    rows = x_ref.shape[0]
    cols = x_ref.shape[1]
    total_x = rows * n_scan
    target = (lax.rem(s + n_scan - STEPS, n_scan), c)
    source = (lax.rem(s + STEPS, n_scan), c)
    f32 = jnp.float32

    barrier = pltpu.get_barrier_semaphore()
    sides = [(ds, dc) for dc in (-1, 1, 0) for ds in (0, -1, 1) if (ds, dc) != (0, 0)]

    def peer(ds, dc):
        return (lax.rem(s + ds + n_scan, n_scan), c + dc)

    def exists(dc):
        if dc < 0:
            return c > 0
        if dc > 0:
            return c < n_cross - 1
        return None

    def guarded(dc, fn):
        cond = exists(dc)
        if cond is None:
            fn()
        else:
            pl.when(cond)(fn)

    for ds, dc in sides:
        def greet(ds=ds, dc=dc):
            pl.semaphore_signal(barrier, 1, device_id=peer(ds, dc), device_id_type=MESH)
        guarded(dc, greet)
    pl.semaphore_signal(barrier, 1, device_id=target, device_id_type=MESH)

    own = pltpu.make_async_copy(
        x_ref, st.at[0, pl.ds(HALO, rows), pl.ds(HALO, cols), :], own_sem
    )
    own.start()

    edges = jnp.where(c > 0, 1, 0) + jnp.where(c < n_cross - 1, 1, 0)
    pl.semaphore_wait(barrier, 3 + 3 * edges)

    def span(d, length, sending):
        if d == 0:
            return pl.ds(0 if sending else HALO, length)
        if d > 0:
            return pl.ds(length - HALO if sending else 0, HALO)
        return pl.ds(0 if sending else HALO + length, HALO)

    copies = {}
    for k, (ds, dc) in enumerate(sides):
        copies[(ds, dc)] = pltpu.make_async_remote_copy(
            src_ref=x_ref.at[span(ds, rows, True), span(dc, cols, True), :],
            dst_ref=st.at[0, span(ds, rows, False), span(dc, cols, False), :],
            send_sem=send_sems.at[k],
            recv_sem=recv_sems.at[k],
            device_id=peer(ds, dc),
            device_id_type=MESH,
        )
    for ds, dc in sides:
        guarded(dc, copies[(ds, dc)].start)

    lane = lax.broadcasted_iota(jnp.int32, (8, 128), 1)
    sub = lax.broadcasted_iota(jnp.int32, (8, 128), 0)
    low = lane < 64
    low_f = jnp.where(low, 1.0, 0.0).astype(f32)
    last_sub = sub == 7
    first_sub = sub == 0
    last_lane = lane == 127
    first_lane = lane == 0
    inner_a = jnp.where(lane < 63, 1.0, 0.0).astype(f32)
    half_coef = [
        jnp.broadcast_to((0.5 * coef_ref[pl.ds(128 * h, 128)])[None, :], (8, 128)) for h in range(2)
    ]
    floor_coef = half_coef[1]

    for t in range(1, LEVELS + 1):
        f = (t - 1) // SUBSTEPS
        n = (t - 1) % SUBSTEPS
        center = (start_ref[f] + n * steps_ref[f]).astype(f32)
        for g in range(4):
            at = sub + (8 * g - HALO) + (s * rows - rows * f + 2 * total_x)
            where_x = lax.rem(at, jnp.int32(total_x)).astype(f32)
            ratio = (where_x - center) * (1.0 / float(rows // 2))
            spot[pl.ds((t - 1) * 32 + 8 * g, 8), :] = jnp.exp(-ratio * ratio)

    z0 = lane.astype(f32)
    absorb = [
        jnp.where(z0 + (128.0 * h) >= 64.0, jnp.exp(-(z0 + (128.0 * h - 64.0)) / absorb_depth), 0.0)
        for h in range(2)
    ]
    for j in range(4):
        col = jnp.zeros((8, 128), f32)
        for i in range(8):
            place = c * cols - HALO + 8 * j + i
            place = jnp.clip(place, 0, n_cross * cols - 1)
            col = jnp.where(sub == i, profile_ref[place], col)
        for h in range(2):
            pa[h, pl.ds(8 * j, 8), :] = heat_power * col * absorb[h]

    left_f = jnp.where(c > 0, 1.0, 0.0).astype(f32)
    right_f = jnp.where(c < n_cross - 1, 1.0, 0.0).astype(f32)
    edge_f = [left_f, None, None, right_f]

    def coupling(t0, t1):
        s0 = t0 * t0
        s1 = t1 * t1
        a = 1.0 + 0.25 * s0
        b = 1.0 + s0
        w = 1.0 / (a * b)
        q0 = b * w
        q1 = 1.0 / (1.0 + 0.25 * s1)
        d = (0.5 * proton_mobility) * s0 * (a * w) * low_f
        return q0, q1, d

    def tile(j):
        return pl.ds(8 * j, 8)

    def init_rows(first, count):
        def body(i, carry):
            X = first + HALO + i
            for j in range(4):
                q0, q1, d = coupling(
                    st[0, X, tile(j), pl.ds(0, 128)], st[0, X, tile(j), pl.ds(128, 128)]
                )
                qb[0, X, tile(j), pl.ds(0, 128)] = q0
                qb[0, X, tile(j), pl.ds(128, 128)] = q1
                db[0, X, tile(j), :] = d
            return carry

        lax.fori_loop(0, count, body, 0)

    def up(tiles):
        rolled = [sub_roll(v, -1) for v in tiles]
        return [
            jnp.where(last_sub, rolled[j + 1], rolled[j]) if j < 3 else rolled[j] for j in range(4)
        ]

    def down(tiles):
        rolled = [sub_roll(v, 1) for v in tiles]
        return [
            jnp.where(first_sub, rolled[j - 1] if j > 0 else 0.0, rolled[j]) for j in range(4)
        ]

    def y_net(vals, facs):
        vu = up(vals)
        fu = up(facs)
        flux = [(facs[j] + fu[j]) * (vu[j] - vals[j]) for j in range(4)]
        flux[3] = jnp.where(last_sub, 0.0, flux[3])
        prev = down(flux)
        return [flux[j] - prev[j] for j in range(4)]

    def block(t, r0):
        a = lax.rem(t + 1, 2)
        b = lax.rem(t, 2)
        X0 = r0 + HALO
        T = {}
        Q = {}
        A = {}
        D = {}
        for i in range(-1, 3):
            for j in range(4):
                for h in range(2):
                    T[i, j, h] = st[a, X0 + i, tile(j), pl.ds(128 * h, 128)]
                    Q[i, j, h] = qb[a, X0 + i, tile(j), pl.ds(128 * h, 128)]
                A[i, j] = st[a, X0 + i, tile(j), pl.ds(256, 128)]
                D[i, j] = db[a, X0 + i, tile(j), :]
        for i in range(2):
            r = r0 + i
            frame = lax.div(t, 2) - 1
            owner = lax.rem(s + lax.div(r + rows, rows) - 1 + n_scan, n_scan)
            wiped = jnp.logical_and(lax.rem(t, 2) == 0, owner == frame)
            keep = jnp.where(wiped, 0.0, 1.0).astype(f32)
            beam = jnp.broadcast_to(spot[pl.ds((t - 1) * 32 + X0 + i, 1), :], (8, 128))
            new = {}
            yn = [
                y_net([T[i, j, h] for j in range(4)], [Q[i, j, h] for j in range(4)])
                for h in range(2)
            ]
            for j in range(4):
                kz = [half_coef[h] * Q[i, j, h] for h in range(2)]
                tr = [lane_roll(T[i, j, h], -1) for h in range(2)]
                kr = [lane_roll(kz[h], -1) for h in range(2)]
                tn = [jnp.where(last_lane, tr[1], tr[0]), jnp.where(last_lane, 0.0, tr[1])]
                kn = [jnp.where(last_lane, kr[1], kr[0]), jnp.where(last_lane, floor_coef, kr[1])]
                fz = [(kz[h] + kn[h]) * (tn[h] - T[i, j, h]) for h in range(2)]
                fr = [lane_roll(fz[h], 1) for h in range(2)]
                fp = [jnp.where(first_lane, 0.0, fr[0]), jnp.where(first_lane, fr[0], fr[1])]
                for h in range(2):
                    cur = T[i, j, h]
                    fx1 = (Q[i, j, h] + Q[i + 1, j, h]) * (T[i + 1, j, h] - cur)
                    fx0 = (Q[i, j, h] + Q[i - 1, j, h]) * (cur - T[i - 1, j, h])
                    lateral = (fx1 - fx0) + yn[h][j]
                    value = cur + (half_coef[h] * lateral + (fz[h] - fp[h]))
                    value = value + beam * pa[h, tile(j), :]
                    scale = keep if edge_f[j] is None else keep * edge_f[j]
                    value = value * scale
                    new[j, h] = value
                    st[b, X0 + i, tile(j), pl.ds(128 * h, 128)] = value
                q0, q1, d = coupling(new[j, 0], new[j, 1])
                qb[b, X0 + i, tile(j), pl.ds(0, 128)] = q0
                qb[b, X0 + i, tile(j), pl.ds(128, 128)] = q1
                db[b, X0 + i, tile(j), :] = d
            ya = y_net([A[i, j] for j in range(4)], [D[i, j] for j in range(4)])
            for j in range(4):
                cur = A[i, j]
                an = lane_roll(cur, -1)
                dn = lane_roll(D[i, j], -1)
                fz = (D[i, j] + dn) * (an - cur) * inner_a
                fx1 = (D[i, j] + D[i + 1, j]) * (A[i + 1, j] - cur)
                fx0 = (D[i, j] + D[i - 1, j]) * (cur - A[i - 1, j])
                value = cur + ((fx1 - fx0) + ya[j] + (fz - lane_roll(fz, 1)))
                if edge_f[j] is not None:
                    value = value * edge_f[j]
                st[b, X0 + i, tile(j), pl.ds(256, 128)] = value

            @pl.when(jnp.logical_and(r >= 0, r < rows))
            def _(i=i, r=r):
                tp = jnp.where(low, T[i, 1, 0], lane_roll(T[i, 2, 0], 64))
                ap = jnp.where(low, A[i, 1], lane_roll(A[i, 2], 64))
                rate = frequency_multiplier * jnp.exp(-barrier_energy / (1.0 + tp))
                pb[r] = pb[r] * (1.0 - rate * ap)

    def march(first_of, count_of, levels):
        def level(t, carry):
            def pair(i, carry):
                block(t, first_of(t) + 2 * i)
                return carry

            lax.fori_loop(0, count_of(t), pair, 0)
            return carry

        lax.fori_loop(1, levels + 1, level, 0)

    def unpack(first, count):
        def body(i, carry):
            X = first + HALO + i
            packed = pb[first + i]
            turned = lane_roll(packed, 64)
            st[0, X, tile(1), pl.ds(256, 128)] = jnp.where(
                low, st[0, X, tile(1), pl.ds(256, 128)], turned
            )
            st[0, X, tile(2), pl.ds(256, 128)] = jnp.where(
                low, st[0, X, tile(2), pl.ds(256, 128)], packed
            )
            return carry

        lax.fori_loop(0, count, body, 0)

    own.wait()

    def pack(i, carry):
        X = HALO + i
        pb[i] = jnp.where(
            low,
            lane_roll(st[0, X, tile(1), pl.ds(256, 128)], 64),
            st[0, X, tile(2), pl.ds(256, 128)],
        )
        return carry

    lax.fori_loop(0, rows, pack, 0)

    def clear(j):
        def body(X, carry):
            for h in range(3):
                st[0, X, tile(j), pl.ds(128 * h, 128)] = jnp.zeros((8, 128), f32)
            return carry

        lax.fori_loop(0, rows + 2 * HALO, body, 0)

    pl.when(c == 0)(lambda: clear(0))
    pl.when(c == n_cross - 1)(lambda: clear(3))

    def arrive(ds):
        for dc in (-1, 0, 1):
            if (ds, dc) != (0, 0):
                k = sides.index((-ds, -dc))
                wait = pltpu.make_async_remote_copy(
                    src_ref=x_ref.at[span(-ds, rows, True), span(-dc, cols, True), :],
                    dst_ref=st.at[0, span(-ds, rows, False), span(-dc, cols, False), :],
                    send_sem=send_sems.at[k],
                    recv_sem=recv_sems.at[k],
                    device_id=peer(ds, dc),
                    device_id_type=MESH,
                )
                guarded(dc, wait.wait_recv)

    def out_copy(part):
        return pltpu.make_async_remote_copy(
            src_ref=st.at[0, pl.ds(HALO + 4 * part, 4), pl.ds(HALO, cols), :],
            dst_ref=o_ref.at[pl.ds(4 * part, 4)],
            send_sem=out_sems.at[part],
            recv_sem=got_sems.at[part],
            device_id=target,
            device_id_type=MESH,
        )

    arrive(0)
    init_rows(0, rows)
    march(lambda t: t, lambda t: 8 - t, LEVELS - 1)
    arrive(-1)
    for part, first in ((1, -4), (0, -8)):
        init_rows(first, 4)
        march(lambda t, first=first: t + first, lambda t: 2, LEVELS)
        unpack(4 * part, 4)
        out_copy(part).start()
    arrive(1)
    for part, first in ((2, 16), (3, 20)):
        init_rows(first, 4)
        march(lambda t, first=first: first - t, lambda t: 2, LEVELS)
        unpack(4 * part, 4)
        out_copy(part).start()
    for part in range(4):
        out_copy(part).wait()
    for ds, dc in sides:
        guarded(dc, copies[(ds, dc)].wait_send)


def shards(wafer_state, layer_heat_coefficients, beam_profile, beam_start, beam_steps):
    smem = pl.BlockSpec(memory_space=pltpu.SMEM)
    f32 = jnp.float32
    rows, cols, chans = wafer_state.shape
    X = rows + 2 * HALO
    Y = cols + 2 * HALO
    return pl.pallas_call(
        kernel,
        out_shape=jax.ShapeDtypeStruct(wafer_state.shape, f32),
        in_specs=[smem, smem, smem, pl.BlockSpec(memory_space=pltpu.VMEM), pl.BlockSpec(memory_space=pl.ANY)],
        out_specs=pl.BlockSpec(memory_space=pl.ANY),
        scratch_shapes=[
            pltpu.VMEM((2, X, Y, chans), f32),
            pltpu.VMEM((2, X, Y, 256), f32),
            pltpu.VMEM((2, X, Y, 128), f32),
            pltpu.VMEM((rows, 8, 128), f32),
            pltpu.VMEM((LEVELS * X, 128), f32),
            pltpu.VMEM((2, Y, 128), f32),
            pltpu.SemaphoreType.DMA((8,)),
            pltpu.SemaphoreType.DMA((8,)),
            pltpu.SemaphoreType.DMA,
            pltpu.SemaphoreType.DMA((4,)),
            pltpu.SemaphoreType.DMA((4,)),
        ],
        compiler_params=pltpu.CompilerParams(collective_id=0, has_side_effects=True),
    )(beam_profile, beam_start, beam_steps, layer_heat_coefficients, wafer_state)


def solution(mesh):
    in_specs = (P("scan", "cross", None), P(), P(), P(), P())
    out_specs = P("scan", "cross", None)
    return jax.shard_map(shards, mesh=mesh, in_specs=in_specs, out_specs=out_specs, check_vma=False)
```

```python
import jax
import jax.numpy as jnp
from jax import lax
from jax.experimental import pallas as pl
from jax.experimental.pallas import tpu as pltpu
from jax.sharding import PartitionSpec as P

STEPS = 4
SUBSTEPS = 2
LEVELS = STEPS * SUBSTEPS
HALO = LEVELS
PAD = 8
PADP = 3
LOG2E = 1.4426950408889634
MESH = pl.DeviceIdType.MESH

heat_power = 0.5
absorb_depth = 6.0
barrier_energy = 3.0
frequency_multiplier = 0.6
proton_mobility = 0.15


def lane_roll(v, shift):
    return pltpu.roll(v, shift % v.shape[1], axis=1)


def kernel(
    profile_ref, start_ref, steps_ref, coef_ref, x_ref, o_ref,
    land, stage, ub0, ub1, kb0, kb1, ab0, ab1, db0, db1, pb, spot, pa, send_sems, recv_sems, own_sem, out_sems, got_sems,
):
    s = lax.axis_index("scan")
    c = lax.axis_index("cross")
    n_scan = lax.axis_size("scan")
    n_cross = lax.axis_size("cross")
    rows = x_ref.shape[0]
    cols = x_ref.shape[1]
    total_x = rows * n_scan
    target = (lax.rem(s + n_scan - STEPS, n_scan), c)
    source = (lax.rem(s + STEPS, n_scan), c)
    f32 = jnp.float32
    ub, kb, ab, db = (ub0, ub1), (kb0, kb1), (ab0, ab1), (db0, db1)

    barrier = pltpu.get_barrier_semaphore()
    sides = [(ds, dc) for dc in (-1, 1, 0) for ds in (0, -1, 1) if (ds, dc) != (0, 0)]

    def peer(ds, dc):
        return (lax.rem(s + ds + n_scan, n_scan), c + dc)

    def exists(dc):
        if dc < 0:
            return c > 0
        if dc > 0:
            return c < n_cross - 1
        return None

    def guarded(dc, fn):
        cond = exists(dc)
        if cond is None:
            fn()
        else:
            pl.when(cond)(fn)

    for ds, dc in sides:
        def greet(ds=ds, dc=dc):
            pl.semaphore_signal(barrier, 1, device_id=peer(ds, dc), device_id_type=MESH)
        guarded(dc, greet)
    pl.semaphore_signal(barrier, 1, device_id=target, device_id_type=MESH)

    own = pltpu.make_async_copy(
        x_ref, land.at[pl.ds(HALO, rows), pl.ds(HALO, cols), :], own_sem
    )
    own.start()

    edges = jnp.where(c > 0, 1, 0) + jnp.where(c < n_cross - 1, 1, 0)
    pl.semaphore_wait(barrier, 3 + 3 * edges)

    def span(d, length, sending):
        if d == 0:
            return pl.ds(0 if sending else HALO, length)
        if d > 0:
            return pl.ds(length - HALO if sending else 0, HALO)
        return pl.ds(0 if sending else HALO + length, HALO)

    copies = {}
    for k, (ds, dc) in enumerate(sides):
        copies[(ds, dc)] = pltpu.make_async_remote_copy(
            src_ref=x_ref.at[span(ds, rows, True), span(dc, cols, True), :],
            dst_ref=land.at[span(ds, rows, False), span(dc, cols, False), :],
            send_sem=send_sems.at[k],
            recv_sem=recv_sems.at[k],
            device_id=peer(ds, dc),
            device_id_type=MESH,
        )
    for ds, dc in sides:
        if ds == 0:
            guarded(dc, copies[(ds, dc)].start)

    lane = lax.broadcasted_iota(jnp.int32, (8, 128), 1)
    sub = lax.broadcasted_iota(jnp.int32, (8, 128), 0)
    low = lane < 64
    last_lane = lane == 127
    first_lane = lane == 0
    half_coef = [
        jnp.broadcast_to((0.5 * coef_ref[pl.ds(128 * h, 128)])[None, :], (8, 128)) for h in range(2)
    ]
    floor_coef = half_coef[1]

    for t in range(1, LEVELS + 1):
        f = (t - 1) // SUBSTEPS
        n = (t - 1) % SUBSTEPS
        center = (start_ref[f] + n * steps_ref[f]).astype(f32)
        for g in range(4):
            at = sub + (8 * g - HALO) + (s * rows - rows * f + 2 * total_x)
            where_x = lax.rem(at, jnp.int32(total_x)).astype(f32)
            ratio = (where_x - center) * (1.0 / float(rows // 2))
            spot[pl.ds((t - 1) * 32 + 8 * g, 8), :] = jnp.exp(-ratio * ratio)

    z0 = lane.astype(f32)
    absorb = [
        jnp.where(z0 + (128.0 * h) >= 64.0, jnp.exp(-(z0 + (128.0 * h - 64.0)) / absorb_depth), 0.0)
        for h in range(2)
    ]
    for j in range(4):
        shine = jnp.zeros((8, 128), f32)
        for i in range(8):
            place = c * cols - HALO + 8 * j + i
            place = jnp.clip(place, 0, n_cross * cols - 1)
            shine = jnp.where(sub == i, profile_ref[place], shine)
        for h in range(2):
            pa[h, pl.ds(8 * j, 8), :] = (0.5 * heat_power) * shine * absorb[h]

    left_f = jnp.where(c > 0, 1.0, 0.0).astype(f32)
    right_f = jnp.where(c < n_cross - 1, 1.0, 0.0).astype(f32)
    edge_f = [left_f, None, None, right_f]
    edge_a = [jnp.where(low, left_f, 1.0), jnp.where(low, 1.0, right_f)]

    def col(j, dy=0):
        return pl.ds(PAD + 8 * j + dy, 8)

    def put_cell(b, X, j, u):
        for h in range(2):
            ub[b][h, X, col(j), :] = u[h]
            kb[b][h, X, col(j), :] = half_coef[h] * (1.0 / (1.0 + u[h] * u[h]))

    def put_acid(b, X, g, acid, u_low, u_high):
        u = jnp.where(low, u_low, lane_roll(u_high, 64))
        sq = u * u
        d = (0.5 * proton_mobility * sq) * (1.0 / (0.25 + sq))
        ghost = pl.ds(PAD + 16, 8) if g == 0 else pl.ds(0, 8)
        ab[b][X, col(g), :] = acid
        ab[b][X, ghost, :] = lane_roll(acid, 64)
        db[b][X, col(g), :] = d
        db[b][X, ghost, :] = lane_roll(d, 64)

    def init_rows(first, count):
        def body(i, carry):
            X = first + HALO + i
            u0 = []
            for j in range(4):
                u = [0.5 * land[X, pl.ds(8 * j, 8), pl.ds(128 * h, 128)] for h in range(2)]
                put_cell(0, X, j, u)
                u0.append(u[0])
            for g in range(2):
                acid = jnp.where(
                    low,
                    land[X, pl.ds(8 * g, 8), pl.ds(256, 128)],
                    lane_roll(land[X, pl.ds(8 * g + 16, 8), pl.ds(256, 128)], 64),
                )
                put_acid(0, X, g, acid, u0[g], u0[g + 2])
            return carry

        lax.fori_loop(0, count, body, 0)

    inner_a = jnp.where(lax.rem(lane, 64) < 63, 1.0, 0.0).astype(f32)

    def block(t, r0, a, b, n):
        X0 = r0 + HALO
        beams = [
            jnp.broadcast_to(spot[pl.ds((t - 1) * 32 + X0 + i, 1), :], (8, 128)) for i in range(n)
        ]

        def side(vals, facs, i, load_v, load_f):
            cur, fac = vals[i], facs[i]
            flux_up = (fac + load_f(i, 1)) * (load_v(i, 1) - cur)
            flux_dn = (fac + load_f(i, -1)) * (cur - load_v(i, -1))
            return flux_up - flux_dn

        def along(vals, facs):
            flux = [(facs[i] + facs[i + 1]) * (vals[i + 1] - vals[i]) for i in range(-1, n)]
            return [flux[i + 1] - flux[i] for i in range(n)]

        fresh = {}
        for g in range(2):
            for j in (g, g + 2):
                U = [
                    {i: ub[a][h, X0 + i, col(j), :] for i in range(-1, n + 1)} for h in range(2)
                ]
                K = [
                    {i: kb[a][h, X0 + i, col(j), :] for i in range(-1, n + 1)} for h in range(2)
                ]
                xn = [along(U[h], K[h]) for h in range(2)]
                for i in range(n):
                    ur = [lane_roll(U[h][i], -1) for h in range(2)]
                    kr = [lane_roll(K[h][i], -1) for h in range(2)]
                    un = [jnp.where(last_lane, ur[1], ur[0]), jnp.where(last_lane, 0.0, ur[1])]
                    kn = [jnp.where(last_lane, kr[1], kr[0]), jnp.where(last_lane, floor_coef, kr[1])]
                    fz = [(K[h][i] + kn[h]) * (un[h] - U[h][i]) for h in range(2)]
                    fr = [lane_roll(fz[h], 1) for h in range(2)]
                    fp = [jnp.where(first_lane, 0.0, fr[0]), jnp.where(first_lane, fr[0], fr[1])]
                    out = []
                    for h in range(2):
                        yn = side(
                            U[h], K[h], i,
                            lambda i, dy, h=h: ub[a][h, X0 + i, col(j, dy), :],
                            lambda i, dy, h=h: kb[a][h, X0 + i, col(j, dy), :],
                        )
                        value = U[h][i] + ((xn[h][i] + yn) + (fz[h] - fp[h]))
                        value = value + beams[i] * pa[h, pl.ds(8 * j, 8), :]
                        if edge_f[j] is not None:
                            value = value * edge_f[j]
                        out.append(value)
                    put_cell(b, X0 + i, j, out)
                    fresh[j, i] = out[0]
            A = {i: ab[a][X0 + i, col(g), :] for i in range(-1, n + 1)}
            D = {i: db[a][X0 + i, col(g), :] for i in range(-1, n + 1)}
            xa = along(A, D)
            for i in range(n):
                fz = ((D[i] + lane_roll(D[i], -1)) * (lane_roll(A[i], -1) - A[i])) * inner_a
                ya = side(
                    A, D, i,
                    lambda i, dy: ab[a][X0 + i, col(g, dy), :],
                    lambda i, dy: db[a][X0 + i, col(g, dy), :],
                )
                value = A[i] + ((xa[i] + ya) + (fz - lane_roll(fz, 1)))
                value = value * edge_a[g]
                put_acid(b, X0 + i, g, value, fresh[g, i], fresh[g + 2, i])

        @pl.when(jnp.logical_and(r0 > -n, r0 < rows))
        def _():
            for i in range(n):
                r = r0 + i + PADP
                tp = jnp.where(
                    low, ub[a][0, X0 + i, col(1), :], lane_roll(ub[a][0, X0 + i, col(2), :], 64)
                )
                ap = jnp.where(low, ab[a][X0 + i, col(1), :], ab[a][X0 + i, col(0), :])
                rate = jnp.exp2((-0.5 * barrier_energy * LOG2E) * (1.0 / (0.5 + tp)))
                pb[r] = pb[r] * (1.0 - (frequency_multiplier * ap) * rate)

        for i in range(n):
            r = r0 + i
            owner = lax.rem(s + lax.div(r + rows, rows) - 1 + n_scan, n_scan)

            if b == 1:
                continue

            @pl.when(owner == lax.div(t, 2) - 1)
            def _(i=i):
                zero = jnp.zeros((8, 128), f32)
                for j in range(4):
                    for h in range(2):
                        ub[b][h, X0 + i, col(j), :] = zero
                        kb[b][h, X0 + i, col(j), :] = half_coef[h]
                for g in range(4):
                    db[b][X0 + i, pl.ds(8 * g, 8), :] = zero

    def levels_in_pairs(level, levels):
        def two(n, carry):
            level(2 * n + 1, 0, 1)
            if levels % 2 == 0:
                level(2 * n + 2, 1, 0)
            else:
                pl.when(2 * n + 2 <= levels)(lambda: level(2 * n + 2, 1, 0))
            return carry

        lax.fori_loop(0, (levels + 1) // 2, two, 0)

    def middle():
        def level(t, a, b):
            def four(i, carry):
                block(t, t + 4 * i, a, b, 4)
                return carry

            lax.fori_loop(0, lax.div(rows - 2 * t, 4), four, 0)
            if b == 1:
                block(t, rows - 2 - t, a, b, 2)

        levels_in_pairs(level, LEVELS - 1)

    def flank(first, slope):
        levels_in_pairs(lambda t, a, b: block(t, first + slope * t, a, b, 4), LEVELS)

    def unpack(first, count):
        def body(i, carry):
            r = first + i
            X = r + HALO
            packed = pb[r + PADP]
            for j in (1, 2):
                for h in range(2):
                    stage[r, pl.ds(8 * j - 8, 8), pl.ds(128 * h, 128)] = 2.0 * ub[0][h, X, col(j), :]
            stage[r, pl.ds(0, 8), pl.ds(256, 128)] = jnp.where(
                low, ab[0][X, col(1), :], lane_roll(packed, 64)
            )
            stage[r, pl.ds(8, 8), pl.ds(256, 128)] = jnp.where(
                low, lane_roll(ab[0][X, col(0), :], 64), packed
            )
            return carry

        lax.fori_loop(0, count, body, 0)

    own.wait()

    def pack(i, carry):
        X = HALO + i
        pb[i + PADP] = jnp.where(
            low,
            lane_roll(land[X, pl.ds(8, 8), pl.ds(256, 128)], 64),
            land[X, pl.ds(16, 8), pl.ds(256, 128)],
        )
        return carry

    lax.fori_loop(0, rows, pack, 0)
    for r in range(PADP):
        pb[r] = jnp.zeros((8, 128), f32)
        pb[rows + PADP + r] = jnp.zeros((8, 128), f32)

    def clear(j):
        def body(X, carry):
            for h in range(3):
                land[X, pl.ds(8 * j, 8), pl.ds(128 * h, 128)] = jnp.zeros((8, 128), f32)
            return carry

        lax.fori_loop(0, rows + 2 * HALO, body, 0)

    pl.when(c == 0)(lambda: clear(0))
    pl.when(c == n_cross - 1)(lambda: clear(3))

    def margins(X, carry):
        for b in range(2):
            for h in range(2):
                for j in (-1, 4):
                    ub[b][h, X, col(j), :] = jnp.zeros((8, 128), f32)
                    kb[b][h, X, col(j), :] = jnp.zeros((8, 128), f32)
        return carry

    lax.fori_loop(0, rows + 2 * HALO, margins, 0)

    def arrive(ds):
        for dc in (-1, 0, 1):
            if (ds, dc) != (0, 0):
                k = sides.index((-ds, -dc))
                wait = pltpu.make_async_remote_copy(
                    src_ref=x_ref.at[span(-ds, rows, True), span(-dc, cols, True), :],
                    dst_ref=land.at[span(-ds, rows, False), span(-dc, cols, False), :],
                    send_sem=send_sems.at[k],
                    recv_sem=recv_sems.at[k],
                    device_id=peer(ds, dc),
                    device_id_type=MESH,
                )
                guarded(dc, wait.wait_recv)

    def out_copy(part):
        return pltpu.make_async_remote_copy(
            src_ref=stage.at[pl.ds(4 * part, 4)],
            dst_ref=o_ref.at[pl.ds(4 * part, 4)],
            send_sem=out_sems.at[part],
            recv_sem=got_sems.at[part],
            device_id=target,
            device_id_type=MESH,
        )

    def finish(part, first, slope):
        init_rows(first, 4)
        flank(first, slope)
        unpack(4 * part, 4)
        out_copy(part).start()

    arrive(0)
    for ds, dc in sides:
        if ds != 0:
            guarded(dc, copies[(ds, dc)].start)
    init_rows(0, rows)
    middle()
    arrive(-1)

    def before(i, carry):
        finish(1 - i, -4 - 4 * i, 1)
        return carry

    def after(i, carry):
        finish(2 + i, rows + 4 * i, -1)
        return carry

    lax.fori_loop(0, 2, before, 0)
    arrive(1)
    lax.fori_loop(0, 2, after, 0)
    for part in range(4):
        out_copy(part).wait()
    for ds, dc in sides:
        guarded(dc, copies[(ds, dc)].wait_send)


def shards(wafer_state, layer_heat_coefficients, beam_profile, beam_start, beam_steps):
    smem = pl.BlockSpec(memory_space=pltpu.SMEM)
    f32 = jnp.float32
    rows, cols, chans = wafer_state.shape
    X = rows + 2 * HALO
    Y = cols + 2 * HALO
    return pl.pallas_call(
        kernel,
        out_shape=jax.ShapeDtypeStruct(wafer_state.shape, f32),
        in_specs=[smem, smem, smem, pl.BlockSpec(memory_space=pltpu.VMEM), pl.BlockSpec(memory_space=pl.ANY)],
        out_specs=pl.BlockSpec(memory_space=pl.ANY),
        scratch_shapes=[
            pltpu.VMEM((X, Y, chans), f32),
            pltpu.VMEM((rows, cols, chans), f32),
            pltpu.VMEM((2, X, Y + 2 * PAD, 128), f32),
            pltpu.VMEM((2, X, Y + 2 * PAD, 128), f32),
            pltpu.VMEM((2, X, Y + 2 * PAD, 128), f32),
            pltpu.VMEM((2, X, Y + 2 * PAD, 128), f32),
            pltpu.VMEM((X, 16 + 2 * PAD, 128), f32),
            pltpu.VMEM((X, 16 + 2 * PAD, 128), f32),
            pltpu.VMEM((X, 16 + 2 * PAD, 128), f32),
            pltpu.VMEM((X, 16 + 2 * PAD, 128), f32),
            pltpu.VMEM((rows + 2 * PADP, 8, 128), f32),
            pltpu.VMEM((LEVELS * X, 128), f32),
            pltpu.VMEM((2, Y, 128), f32),
            pltpu.SemaphoreType.DMA((8,)),
            pltpu.SemaphoreType.DMA((8,)),
            pltpu.SemaphoreType.DMA,
            pltpu.SemaphoreType.DMA((4,)),
            pltpu.SemaphoreType.DMA((4,)),
        ],
        compiler_params=pltpu.CompilerParams(collective_id=0, has_side_effects=True),
    )(beam_profile, beam_start, beam_steps, layer_heat_coefficients, wafer_state)


def solution(mesh):
    in_specs = (P("scan", "cross", None), P(), P(), P(), P())
    out_specs = P("scan", "cross", None)
    return jax.shard_map(shards, mesh=mesh, in_specs=in_specs, out_specs=out_specs, check_vma=False)
```

```python
import jax
import jax.numpy as jnp
from jax import lax
from jax.experimental import pallas as pl
from jax.experimental.pallas import tpu as pltpu
from jax.sharding import PartitionSpec as P

STEPS = 4
SUBSTEPS = 2
LEVELS = STEPS * SUBSTEPS
HALO = LEVELS
REACH = LEVELS // 2
PAD = 8
PADP = 3
LOG2E = 1.4426950408889634
MESH = pl.DeviceIdType.MESH

heat_power = 0.5
absorb_depth = 6.0
barrier_energy = 3.0
frequency_multiplier = 0.6
proton_mobility = 0.15


def lane_roll(v, shift):
    return pltpu.roll(v, shift % v.shape[1], axis=1)


def kernel(
    profile_ref, start_ref, steps_ref, coef_ref, x_ref, o_ref,
    land, stage, send_u, send_a, land_u, land_a, ub0, ub1, kb0, kb1, ab0, ab1, db0, db1, pb, spot, pa, send_sems, recv_sems, own_sem, out_sems, got_sems,
    mid_send_sems, mid_recv_sems,
):
    s = lax.axis_index("scan")
    c = lax.axis_index("cross")
    n_scan = lax.axis_size("scan")
    n_cross = lax.axis_size("cross")
    rows = x_ref.shape[0]
    cols = x_ref.shape[1]
    total_x = rows * n_scan
    target = (lax.rem(s + n_scan - STEPS, n_scan), c)
    source = (lax.rem(s + STEPS, n_scan), c)
    f32 = jnp.float32
    ub, kb, ab, db = (ub0, ub1), (kb0, kb1), (ab0, ab1), (db0, db1)

    barrier = pltpu.get_barrier_semaphore()
    sides = [(ds, dc) for dc in (-1, 1, 0) for ds in (0, -1, 1) if (ds, dc) != (0, 0)]

    def peer(ds, dc):
        return (lax.rem(s + ds + n_scan, n_scan), c + dc)

    def exists(dc):
        if dc < 0:
            return c > 0
        if dc > 0:
            return c < n_cross - 1
        return None

    def guarded(dc, fn):
        cond = exists(dc)
        if cond is None:
            fn()
        else:
            pl.when(cond)(fn)

    for ds, dc in sides:
        def greet(ds=ds, dc=dc):
            pl.semaphore_signal(barrier, 1, device_id=peer(ds, dc), device_id_type=MESH)
        guarded(dc, greet)
    pl.semaphore_signal(barrier, 1, device_id=target, device_id_type=MESH)

    own = pltpu.make_async_copy(
        x_ref, land.at[pl.ds(REACH, rows), pl.ds(HALO, cols), :], own_sem
    )
    own.start()

    edges = jnp.where(c > 0, 1, 0) + jnp.where(c < n_cross - 1, 1, 0)
    pl.semaphore_wait(barrier, 3 + 3 * edges)

    def span(d, length, sending, halo):
        if d == 0:
            return pl.ds(0 if sending else halo, length)
        if d > 0:
            return pl.ds(length - halo if sending else 0, halo)
        return pl.ds(0 if sending else halo + length, halo)

    copies = {}
    for k, (ds, dc) in enumerate(sides):
        copies[(ds, dc)] = pltpu.make_async_remote_copy(
            src_ref=x_ref.at[span(ds, rows, True, REACH), span(dc, cols, True, HALO), :],
            dst_ref=land.at[span(ds, rows, False, REACH), span(dc, cols, False, HALO), :],
            send_sem=send_sems.at[k],
            recv_sem=recv_sems.at[k],
            device_id=peer(ds, dc),
            device_id_type=MESH,
        )
    for ds, dc in sides:
        if ds == 0:
            guarded(dc, copies[(ds, dc)].start)

    lane = lax.broadcasted_iota(jnp.int32, (8, 128), 1)
    sub = lax.broadcasted_iota(jnp.int32, (8, 128), 0)
    low = lane < 64
    last_lane = lane == 127
    first_lane = lane == 0
    half_coef = [
        jnp.broadcast_to((0.5 * coef_ref[pl.ds(128 * h, 128)])[None, :], (8, 128)) for h in range(2)
    ]
    floor_coef = half_coef[1]

    for t in range(1, LEVELS + 1):
        f = (t - 1) // SUBSTEPS
        n = (t - 1) % SUBSTEPS
        center = (start_ref[f] + n * steps_ref[f]).astype(f32)
        for g in range(3):
            at = sub + (8 * g - REACH) + (s * rows - rows * f + 2 * total_x)
            where_x = lax.rem(at, jnp.int32(total_x)).astype(f32)
            ratio = (where_x - center) * (1.0 / float(rows // 2))
            spot[pl.ds((t - 1) * 24 + 8 * g, 8), :] = jnp.exp(-ratio * ratio)

    z0 = lane.astype(f32)
    absorb = [
        jnp.where(z0 + (128.0 * h) >= 64.0, jnp.exp(-(z0 + (128.0 * h - 64.0)) / absorb_depth), 0.0)
        for h in range(2)
    ]
    for j in range(4):
        shine = jnp.zeros((8, 128), f32)
        for i in range(8):
            place = c * cols - HALO + 8 * j + i
            place = jnp.clip(place, 0, n_cross * cols - 1)
            shine = jnp.where(sub == i, profile_ref[place], shine)
        for h in range(2):
            pa[h, pl.ds(8 * j, 8), :] = (0.5 * heat_power) * shine * absorb[h]

    left_f = jnp.where(c > 0, 1.0, 0.0).astype(f32)
    right_f = jnp.where(c < n_cross - 1, 1.0, 0.0).astype(f32)
    edge_f = [left_f, None, None, right_f]
    edge_a = [jnp.where(low, left_f, 1.0), jnp.where(low, 1.0, right_f)]

    def col(j, dy=0):
        return pl.ds(PAD + 8 * j + dy, 8)

    def put_cell(b, X, j, u):
        for h in range(2):
            ub[b][h, X, col(j), :] = u[h]
            kb[b][h, X, col(j), :] = half_coef[h] * (1.0 / (1.0 + u[h] * u[h]))

    def put_acid(b, X, g, acid, u_low, u_high):
        u = jnp.where(low, u_low, lane_roll(u_high, 64))
        sq = u * u
        d = (0.5 * proton_mobility * sq) * (1.0 / (0.25 + sq))
        ghost = pl.ds(PAD + 16, 8) if g == 0 else pl.ds(0, 8)
        ab[b][X, col(g), :] = acid
        ab[b][X, ghost, :] = lane_roll(acid, 64)
        db[b][X, col(g), :] = d
        db[b][X, ghost, :] = lane_roll(d, 64)

    def init_rows(first, count):
        def body(i, carry):
            X = first + REACH + i
            u0 = []
            for j in range(4):
                u = [0.5 * land[X, pl.ds(8 * j, 8), pl.ds(128 * h, 128)] for h in range(2)]
                put_cell(0, X, j, u)
                u0.append(u[0])
            for g in range(2):
                acid = jnp.where(
                    low,
                    land[X, pl.ds(8 * g, 8), pl.ds(256, 128)],
                    lane_roll(land[X, pl.ds(8 * g + 16, 8), pl.ds(256, 128)], 64),
                )
                put_acid(0, X, g, acid, u0[g], u0[g + 2])
            return carry

        lax.fori_loop(0, count, body, 0)

    inner_a = jnp.where(lax.rem(lane, 64) < 63, 1.0, 0.0).astype(f32)

    def block(t, r0, a, b, n):
        X0 = r0 + REACH
        beams = [
            jnp.broadcast_to(spot[pl.ds((t - 1) * 24 + X0 + i, 1), :], (8, 128)) for i in range(n)
        ]

        def side(vals, facs, i, load_v, load_f):
            cur, fac = vals[i], facs[i]
            flux_up = (fac + load_f(i, 1)) * (load_v(i, 1) - cur)
            flux_dn = (fac + load_f(i, -1)) * (cur - load_v(i, -1))
            return flux_up - flux_dn

        def along(vals, facs):
            flux = [(facs[i] + facs[i + 1]) * (vals[i + 1] - vals[i]) for i in range(-1, n)]
            return [flux[i + 1] - flux[i] for i in range(n)]

        fresh = {}
        for g in range(2):
            for j in (g, g + 2):
                U = [
                    {i: ub[a][h, X0 + i, col(j), :] for i in range(-1, n + 1)} for h in range(2)
                ]
                K = [
                    {i: kb[a][h, X0 + i, col(j), :] for i in range(-1, n + 1)} for h in range(2)
                ]
                xn = [along(U[h], K[h]) for h in range(2)]
                for i in range(n):
                    ur = [lane_roll(U[h][i], -1) for h in range(2)]
                    kr = [lane_roll(K[h][i], -1) for h in range(2)]
                    un = [jnp.where(last_lane, ur[1], ur[0]), jnp.where(last_lane, 0.0, ur[1])]
                    kn = [jnp.where(last_lane, kr[1], kr[0]), jnp.where(last_lane, floor_coef, kr[1])]
                    fz = [(K[h][i] + kn[h]) * (un[h] - U[h][i]) for h in range(2)]
                    fr = [lane_roll(fz[h], 1) for h in range(2)]
                    fp = [jnp.where(first_lane, 0.0, fr[0]), jnp.where(first_lane, fr[0], fr[1])]
                    out = []
                    for h in range(2):
                        yn = side(
                            U[h], K[h], i,
                            lambda i, dy, h=h: ub[a][h, X0 + i, col(j, dy), :],
                            lambda i, dy, h=h: kb[a][h, X0 + i, col(j, dy), :],
                        )
                        value = U[h][i] + ((xn[h][i] + yn) + (fz[h] - fp[h]))
                        value = value + beams[i] * pa[h, pl.ds(8 * j, 8), :]
                        if edge_f[j] is not None:
                            value = value * edge_f[j]
                        out.append(value)
                    put_cell(b, X0 + i, j, out)
                    fresh[j, i] = out[0]
            A = {i: ab[a][X0 + i, col(g), :] for i in range(-1, n + 1)}
            D = {i: db[a][X0 + i, col(g), :] for i in range(-1, n + 1)}
            xa = along(A, D)
            for i in range(n):
                fz = ((D[i] + lane_roll(D[i], -1)) * (lane_roll(A[i], -1) - A[i])) * inner_a
                ya = side(
                    A, D, i,
                    lambda i, dy: ab[a][X0 + i, col(g, dy), :],
                    lambda i, dy: db[a][X0 + i, col(g, dy), :],
                )
                value = A[i] + ((xa[i] + ya) + (fz - lane_roll(fz, 1)))
                value = value * edge_a[g]
                put_acid(b, X0 + i, g, value, fresh[g, i], fresh[g + 2, i])

        @pl.when(jnp.logical_and(r0 > -n, r0 < rows))
        def _():
            for i in range(n):
                r = r0 + i + PADP
                tp = jnp.where(
                    low, ub[a][0, X0 + i, col(1), :], lane_roll(ub[a][0, X0 + i, col(2), :], 64)
                )
                ap = jnp.where(low, ab[a][X0 + i, col(1), :], ab[a][X0 + i, col(0), :])
                rate = jnp.exp2((-0.5 * barrier_energy * LOG2E) * (1.0 / (0.5 + tp)))
                pb[r] = pb[r] * (1.0 - (frequency_multiplier * ap) * rate)

        for i in range(n):
            r = r0 + i
            owner = lax.rem(s + lax.div(r + rows, rows) - 1 + n_scan, n_scan)

            if b == 1:
                continue

            @pl.when(owner == lax.div(t, 2) - 1)
            def _(i=i):
                zero = jnp.zeros((8, 128), f32)
                for j in range(4):
                    for h in range(2):
                        ub[b][h, X0 + i, col(j), :] = zero
                        kb[b][h, X0 + i, col(j), :] = half_coef[h]
                for g in range(4):
                    db[b][X0 + i, pl.ds(8 * g, 8), :] = zero

    def levels_in_pairs(level, base):
        def two(m, carry):
            level(2 * m + 1, base + 2 * m + 1, 0, 1)
            level(2 * m + 2, base + 2 * m + 2, 1, 0)
            return carry

        lax.fori_loop(0, REACH // 2, two, 0)

    def middle(base):
        def level(k, t, a, b):
            def four(i, carry):
                block(t, k + 4 * i, a, b, 4)
                return carry

            lax.fori_loop(0, lax.div(rows - 2 * k, 4), four, 0)
            if b == 1:
                block(t, rows - 2 - k, a, b, 2)

        levels_in_pairs(level, base)

    def flank(base, first, slope):
        levels_in_pairs(lambda k, t, a, b: block(t, first + slope * k, a, b, 4), base)

    def unpack(first, count):
        def body(i, carry):
            r = first + i
            X = r + REACH
            packed = pb[r + PADP]
            for j in (1, 2):
                for h in range(2):
                    stage[r, pl.ds(8 * j - 8, 8), pl.ds(128 * h, 128)] = 2.0 * ub[0][h, X, col(j), :]
            stage[r, pl.ds(0, 8), pl.ds(256, 128)] = jnp.where(
                low, ab[0][X, col(1), :], lane_roll(packed, 64)
            )
            stage[r, pl.ds(8, 8), pl.ds(256, 128)] = jnp.where(
                low, lane_roll(ab[0][X, col(0), :], 64), packed
            )
            return carry

        lax.fori_loop(0, count, body, 0)

    own.wait()

    def pack(i, carry):
        X = REACH + i
        pb[i + PADP] = jnp.where(
            low,
            lane_roll(land[X, pl.ds(8, 8), pl.ds(256, 128)], 64),
            land[X, pl.ds(16, 8), pl.ds(256, 128)],
        )
        return carry

    lax.fori_loop(0, rows, pack, 0)
    for r in range(PADP):
        pb[r] = jnp.zeros((8, 128), f32)
        pb[rows + PADP + r] = jnp.zeros((8, 128), f32)

    def clear(j):
        def body(X, carry):
            for h in range(3):
                land[X, pl.ds(8 * j, 8), pl.ds(128 * h, 128)] = jnp.zeros((8, 128), f32)
            return carry

        lax.fori_loop(0, rows + 2 * REACH, body, 0)

    pl.when(c == 0)(lambda: clear(0))
    pl.when(c == n_cross - 1)(lambda: clear(3))

    def margins(X, carry):
        for b in range(2):
            for h in range(2):
                for j in (-1, 4):
                    ub[b][h, X, col(j), :] = jnp.zeros((8, 128), f32)
                    kb[b][h, X, col(j), :] = jnp.zeros((8, 128), f32)
        return carry

    lax.fori_loop(0, rows + 2 * REACH, margins, 0)

    def arrive(ds):
        for dc in (-1, 0, 1):
            if (ds, dc) != (0, 0):
                k = sides.index((-ds, -dc))
                wait = pltpu.make_async_remote_copy(
                    src_ref=x_ref.at[span(-ds, rows, True, REACH), span(-dc, cols, True, HALO), :],
                    dst_ref=land.at[span(-ds, rows, False, REACH), span(-dc, cols, False, HALO), :],
                    send_sem=send_sems.at[k],
                    recv_sem=recv_sems.at[k],
                    device_id=peer(ds, dc),
                    device_id_type=MESH,
                )
                guarded(dc, wait.wait_recv)

    def out_copy(part):
        return pltpu.make_async_remote_copy(
            src_ref=stage.at[pl.ds(4 * part, 4)],
            dst_ref=o_ref.at[pl.ds(4 * part, 4)],
            send_sem=out_sems.at[part],
            recv_sem=got_sems.at[part],
            device_id=target,
            device_id_type=MESH,
        )

    def finish(part, first, slope):
        init_rows(first, 4)
        flank(first, slope)
        unpack(4 * part, 4)
        out_copy(part).start()

    def mid_copies(side):
        to = peer(2 * side - 1, 0)
        return [
            pltpu.make_async_remote_copy(
                src_ref=src.at[side],
                dst_ref=dst.at[1 - side],
                send_sem=mid_send_sems.at[2 * side + n],
                recv_sem=mid_recv_sems.at[2 * side + n],
                device_id=to,
                device_id_type=MESH,
            )
            for n, (src, dst) in enumerate(((send_u, land_u), (send_a, land_a)))
        ]

    def give(side):
        for i in range(REACH):
            X = REACH + i + side * (rows - REACH)
            for j in range(4):
                for h in range(2):
                    send_u[side, h, i, pl.ds(8 * j, 8), :] = ub[0][h, X, col(j), :]
            for g in range(2):
                send_a[side, i, pl.ds(8 * g, 8), :] = ab[0][X, col(g), :]
        for copy in mid_copies(side):
            copy.start()

    def take(side):
        for copy in mid_copies(1 - side):
            copy.wait_recv()

        def body(i, carry):
            X = i + side * (rows + REACH)
            u0 = []
            for j in range(4):
                u = [land_u[side, h, i, pl.ds(8 * j, 8), :] for h in range(2)]
                put_cell(0, X, j, u)
                u0.append(u[0])
            for g in range(2):
                put_acid(0, X, g, land_a[side, i, pl.ds(8 * g, 8), :], u0[g], u0[g + 2])
            return carry

        lax.fori_loop(0, REACH, body, 0)

    def finish(part):
        unpack(4 * part, 4)
        out_copy(part).start()

    arrive(0)
    for ds, dc in sides:
        if ds != 0:
            guarded(dc, copies[(ds, dc)].start)
    init_rows(0, rows)
    middle(0)
    arrive(-1)
    init_rows(-4, 4)
    flank(0, -4, 1)
    give(0)
    arrive(1)
    init_rows(rows, 4)
    flank(0, rows, -1)
    give(1)
    middle(REACH)
    finish(1)
    finish(2)
    take(0)
    flank(REACH, -4, 1)
    finish(0)
    take(1)
    flank(REACH, rows, -1)
    finish(3)
    for part in range(4):
        out_copy(part).wait()
    for side in range(2):
        for copy in mid_copies(side):
            copy.wait_send()
    for ds, dc in sides:
        guarded(dc, copies[(ds, dc)].wait_send)


def shards(wafer_state, layer_heat_coefficients, beam_profile, beam_start, beam_steps):
    smem = pl.BlockSpec(memory_space=pltpu.SMEM)
    f32 = jnp.float32
    rows, cols, chans = wafer_state.shape
    X = rows + 2 * REACH
    Y = cols + 2 * HALO
    return pl.pallas_call(
        kernel,
        out_shape=jax.ShapeDtypeStruct(wafer_state.shape, f32),
        in_specs=[smem, smem, smem, pl.BlockSpec(memory_space=pltpu.VMEM), pl.BlockSpec(memory_space=pl.ANY)],
        out_specs=pl.BlockSpec(memory_space=pl.ANY),
        scratch_shapes=[
            pltpu.VMEM((X, Y, chans), f32),
            pltpu.VMEM((rows, cols, chans), f32),
            pltpu.VMEM((2, 2, REACH, Y, 128), f32),
            pltpu.VMEM((2, REACH, 16, 128), f32),
            pltpu.VMEM((2, 2, REACH, Y, 128), f32),
            pltpu.VMEM((2, REACH, 16, 128), f32),
            pltpu.VMEM((2, X, Y + 2 * PAD, 128), f32),
            pltpu.VMEM((2, X, Y + 2 * PAD, 128), f32),
            pltpu.VMEM((2, X, Y + 2 * PAD, 128), f32),
            pltpu.VMEM((2, X, Y + 2 * PAD, 128), f32),
            pltpu.VMEM((X, 16 + 2 * PAD, 128), f32),
            pltpu.VMEM((X, 16 + 2 * PAD, 128), f32),
            pltpu.VMEM((X, 16 + 2 * PAD, 128), f32),
            pltpu.VMEM((X, 16 + 2 * PAD, 128), f32),
            pltpu.VMEM((rows + 2 * PADP, 8, 128), f32),
            pltpu.VMEM((LEVELS * 24, 128), f32),
            pltpu.VMEM((2, Y, 128), f32),
            pltpu.SemaphoreType.DMA((8,)),
            pltpu.SemaphoreType.DMA((8,)),
            pltpu.SemaphoreType.DMA,
            pltpu.SemaphoreType.DMA((4,)),
            pltpu.SemaphoreType.DMA((4,)),
            pltpu.SemaphoreType.DMA((4,)),
            pltpu.SemaphoreType.DMA((4,)),
        ],
        compiler_params=pltpu.CompilerParams(collective_id=0, has_side_effects=True),
    )(beam_profile, beam_start, beam_steps, layer_heat_coefficients, wafer_state)


def solution(mesh):
    in_specs = (P("scan", "cross", None), P(), P(), P(), P())
    out_specs = P("scan", "cross", None)
    return jax.shard_map(shards, mesh=mesh, in_specs=in_specs, out_specs=out_specs, check_vma=False)
```

```python
import jax
import jax.numpy as jnp
from jax import lax
from jax.experimental import pallas as pl
from jax.experimental.pallas import tpu as pltpu
from jax.sharding import PartitionSpec as P

STEPS = 4
SUBSTEPS = 2
LEVELS = STEPS * SUBSTEPS
HALO = LEVELS
REACH = LEVELS // 2
PAD = 8
LOG2E = 1.4426950408889634
MESH = pl.DeviceIdType.MESH

heat_power = 0.5
absorb_depth = 6.0
barrier_energy = 3.0
frequency_multiplier = 0.6
proton_mobility = 0.15


def lane_roll(v, shift):
    return pltpu.roll(v, shift % v.shape[1], axis=1)


def kernel(
    profile_ref, start_ref, steps_ref, coef_ref, x_ref, o_ref,
    land, stage, send_u, send_a, land_u, land_a, ub0, ub1, kb0, kb1, ab0, ab1, db0, db1, pb, spot, pa, send_sems, recv_sems, own_sem, out_sems, got_sems,
    mid_send_sems, mid_recv_sems,
):
    s = lax.axis_index("scan")
    c = lax.axis_index("cross")
    n_scan = lax.axis_size("scan")
    n_cross = lax.axis_size("cross")
    rows = x_ref.shape[0]
    cols = x_ref.shape[1]
    total_x = rows * n_scan
    target = (lax.rem(s + n_scan - STEPS, n_scan), c)
    source = (lax.rem(s + STEPS, n_scan), c)
    f32 = jnp.float32
    ub, kb, ab, db = (ub0, ub1), (kb0, kb1), (ab0, ab1), (db0, db1)

    barrier = pltpu.get_barrier_semaphore()
    sides = [(0, -1), (0, 1), (-1, 0), (1, 0)]

    def peer(ds, dc):
        return (lax.rem(s + ds + n_scan, n_scan), c + dc)

    def exists(dc):
        if dc < 0:
            return c > 0
        if dc > 0:
            return c < n_cross - 1
        return None

    def guarded(dc, fn):
        cond = exists(dc)
        if cond is None:
            fn()
        else:
            pl.when(cond)(fn)

    for ds, dc in sides:
        def greet(ds=ds, dc=dc):
            pl.semaphore_signal(barrier, 1, device_id=peer(ds, dc), device_id_type=MESH)
        guarded(dc, greet)
    pl.semaphore_signal(barrier, 1, device_id=target, device_id_type=MESH)

    own = pltpu.make_async_copy(
        x_ref, land.at[pl.ds(REACH, rows), pl.ds(HALO, cols), :], own_sem
    )
    own.start()

    def span(d, length, sending, halo):
        if d == 0:
            return pl.ds(0 if sending else halo, length)
        if d > 0:
            return pl.ds(length - halo if sending else 0, halo)
        return pl.ds(0 if sending else halo + length, halo)

    def halo_copy(ds, dc):
        k = sides.index((ds, dc))
        if ds == 0:
            source_ref = x_ref.at[:, span(dc, cols, True, HALO), :]
            landing = land.at[pl.ds(REACH, rows), span(dc, cols, False, HALO), :]
        else:
            source_ref = land.at[pl.ds(REACH if ds < 0 else rows, REACH)]
            landing = land.at[span(ds, rows, False, REACH)]
        return pltpu.make_async_remote_copy(
            src_ref=source_ref,
            dst_ref=landing,
            send_sem=send_sems.at[k],
            recv_sem=recv_sems.at[k],
            device_id=peer(ds, dc),
            device_id_type=MESH,
        )

    lane = lax.broadcasted_iota(jnp.int32, (8, 128), 1)
    sub = lax.broadcasted_iota(jnp.int32, (8, 128), 0)
    low = lane < 64
    last_lane = lane == 127
    first_lane = lane == 0
    half_coef = [
        jnp.broadcast_to((0.5 * coef_ref[pl.ds(128 * h, 128)])[None, :], (8, 128)) for h in range(2)
    ]
    floor_coef = half_coef[1]

    for t in range(1, LEVELS + 1):
        f = (t - 1) // SUBSTEPS
        n = (t - 1) % SUBSTEPS
        center = (start_ref[f] + n * steps_ref[f]).astype(f32)
        for g in range(3):
            at = sub + (8 * g - REACH) + (s * rows - rows * f + 2 * total_x)
            where_x = lax.rem(at, jnp.int32(total_x)).astype(f32)
            ratio = (where_x - center) * (1.0 / float(rows // 2))
            spot[pl.ds((t - 1) * 24 + 8 * g, 8), :] = jnp.exp(-ratio * ratio)

    z0 = lane.astype(f32)
    absorb = [
        jnp.where(z0 + (128.0 * h) >= 64.0, jnp.exp(-(z0 + (128.0 * h - 64.0)) / absorb_depth), 0.0)
        for h in range(2)
    ]
    for j in range(4):
        shine = jnp.zeros((8, 128), f32)
        for i in range(8):
            place = c * cols - HALO + 8 * j + i
            place = jnp.clip(place, 0, n_cross * cols - 1)
            shine = jnp.where(sub == i, profile_ref[place], shine)
        for h in range(2):
            pa[h, pl.ds(8 * j, 8), :] = (0.5 * heat_power) * shine * absorb[h]

    left_f = jnp.where(c > 0, 1.0, 0.0).astype(f32)
    right_f = jnp.where(c < n_cross - 1, 1.0, 0.0).astype(f32)
    edge_f = [left_f, None, None, right_f]
    edge_a = [jnp.where(low, left_f, 1.0), jnp.where(low, 1.0, right_f)]

    def col(j, dy=0):
        return pl.ds(PAD + 8 * j + dy, 8)

    def put_cell(b, X, j, u):
        for h in range(2):
            ub[b][h, X, col(j), :] = u[h]
            kb[b][h, X, col(j), :] = half_coef[h] * (1.0 / (1.0 + u[h] * u[h]))

    def put_acid(b, X, g, acid, u_low, u_high):
        u = jnp.where(low, u_low, lane_roll(u_high, 64))
        sq = u * u
        d = (0.5 * proton_mobility * sq) * (1.0 / (0.25 + sq))
        ghost = pl.ds(PAD + 16, 8) if g == 0 else pl.ds(0, 8)
        ab[b][X, col(g), :] = acid
        ab[b][X, ghost, :] = lane_roll(acid, 64)
        db[b][X, col(g), :] = d
        db[b][X, ghost, :] = lane_roll(d, 64)

    def init_rows(first, count):
        def body(q, carry):
            for i in range(4):
                X = first + REACH + 4 * q + i
                u0 = []
                for j in range(4):
                    u = [0.5 * land[X, pl.ds(8 * j, 8), pl.ds(128 * h, 128)] for h in range(2)]
                    put_cell(0, X, j, u)
                    u0.append(u[0])
                last = [land[X, pl.ds(8 * j, 8), pl.ds(256, 128)] for j in range(4)]
                for g in range(2):
                    acid = jnp.where(low, last[g], lane_roll(last[g + 2], 64))
                    put_acid(0, X, g, acid, u0[g], u0[g + 2])
                pb[X] = jnp.where(low, lane_roll(last[1], 64), last[2])
            return carry

        lax.fori_loop(0, count // 4, body, 0)

    inner_a = jnp.where(lax.rem(lane, 64) < 63, 1.0, 0.0).astype(f32)

    def block(t, r0, a, b, n):
        X0 = r0 + REACH
        beams = [
            jnp.broadcast_to(spot[pl.ds((t - 1) * 24 + X0 + i, 1), :], (8, 128)) for i in range(n)
        ]

        def side(vals, facs, i, load_v, load_f):
            cur, fac = vals[i], facs[i]
            flux_up = (fac + load_f(i, 1)) * (load_v(i, 1) - cur)
            flux_dn = (fac + load_f(i, -1)) * (cur - load_v(i, -1))
            return flux_up - flux_dn

        def along(vals, facs):
            flux = [(facs[i] + facs[i + 1]) * (vals[i + 1] - vals[i]) for i in range(-1, n)]
            return [flux[i + 1] - flux[i] for i in range(n)]

        fresh = {}
        for g in range(2):
            for j in (g, g + 2):
                U = [
                    {i: ub[a][h, X0 + i, col(j), :] for i in range(-1, n + 1)} for h in range(2)
                ]
                K = [
                    {i: kb[a][h, X0 + i, col(j), :] for i in range(-1, n + 1)} for h in range(2)
                ]
                xn = [along(U[h], K[h]) for h in range(2)]
                for i in range(n):
                    ur = [lane_roll(U[h][i], -1) for h in range(2)]
                    kr = [lane_roll(K[h][i], -1) for h in range(2)]
                    un = [jnp.where(last_lane, ur[1], ur[0]), jnp.where(last_lane, 0.0, ur[1])]
                    kn = [jnp.where(last_lane, kr[1], kr[0]), jnp.where(last_lane, floor_coef, kr[1])]
                    fz = [(K[h][i] + kn[h]) * (un[h] - U[h][i]) for h in range(2)]
                    fr = [lane_roll(fz[h], 1) for h in range(2)]
                    fp = [jnp.where(first_lane, 0.0, fr[0]), jnp.where(first_lane, fr[0], fr[1])]
                    out = []
                    for h in range(2):
                        yn = side(
                            U[h], K[h], i,
                            lambda i, dy, h=h: ub[a][h, X0 + i, col(j, dy), :],
                            lambda i, dy, h=h: kb[a][h, X0 + i, col(j, dy), :],
                        )
                        value = U[h][i] + ((xn[h][i] + yn) + (fz[h] - fp[h]))
                        value = value + beams[i] * pa[h, pl.ds(8 * j, 8), :]
                        if edge_f[j] is not None:
                            value = value * edge_f[j]
                        out.append(value)
                    put_cell(b, X0 + i, j, out)
                    fresh[j, i] = out[0]
            A = {i: ab[a][X0 + i, col(g), :] for i in range(-1, n + 1)}
            D = {i: db[a][X0 + i, col(g), :] for i in range(-1, n + 1)}
            xa = along(A, D)
            for i in range(n):
                fz = ((D[i] + lane_roll(D[i], -1)) * (lane_roll(A[i], -1) - A[i])) * inner_a
                ya = side(
                    A, D, i,
                    lambda i, dy: ab[a][X0 + i, col(g, dy), :],
                    lambda i, dy: db[a][X0 + i, col(g, dy), :],
                )
                value = A[i] + ((xa[i] + ya) + (fz - lane_roll(fz, 1)))
                value = value * edge_a[g]
                put_acid(b, X0 + i, g, value, fresh[g, i], fresh[g + 2, i])

        @pl.when(jnp.logical_and(r0 > -n, r0 < rows))
        def _():
            for i in range(n):
                tp = jnp.where(
                    low, ub[a][0, X0 + i, col(1), :], lane_roll(ub[a][0, X0 + i, col(2), :], 64)
                )
                ap = jnp.where(low, ab[a][X0 + i, col(1), :], ab[a][X0 + i, col(0), :])
                rate = jnp.exp2((-0.5 * barrier_energy * LOG2E) * (1.0 / (0.5 + tp)))
                pb[X0 + i] = pb[X0 + i] * (1.0 - (frequency_multiplier * ap) * rate)

        for i in range(n):
            r = r0 + i
            owner = lax.rem(s + lax.div(r + rows, rows) - 1 + n_scan, n_scan)

            if b == 1:
                continue

            @pl.when(owner == lax.div(t, 2) - 1)
            def _(i=i):
                zero = jnp.zeros((8, 128), f32)
                for j in range(4):
                    for h in range(2):
                        ub[b][h, X0 + i, col(j), :] = zero
                        kb[b][h, X0 + i, col(j), :] = half_coef[h]
                for g in range(4):
                    db[b][X0 + i, pl.ds(8 * g, 8), :] = zero

    def levels_in_pairs(level, base):
        def two(m, carry):
            level(2 * m + 1, base + 2 * m + 1, 0, 1)
            level(2 * m + 2, base + 2 * m + 2, 1, 0)
            return carry

        lax.fori_loop(0, REACH // 2, two, 0)

    def middle(base):
        def level(k, t, a, b):
            def four(i, carry):
                block(t, k + 4 * i, a, b, 4)
                return carry

            lax.fori_loop(0, lax.div(rows - 2 * k, 4), four, 0)
            if b == 1:
                block(t, rows - 2 - k, a, b, 2)

        levels_in_pairs(level, base)

    def flank(base, first, slope):
        levels_in_pairs(lambda k, t, a, b: block(t, first + slope * k, a, b, 4), base)

    def unpack(first, count):
        for i in range(count):
            r = first + i
            X = r + REACH
            packed = pb[X]
            for j in (1, 2):
                for h in range(2):
                    stage[r, pl.ds(8 * j - 8, 8), pl.ds(128 * h, 128)] = 2.0 * ub[0][h, X, col(j), :]
            stage[r, pl.ds(0, 8), pl.ds(256, 128)] = jnp.where(
                low, ab[0][X, col(1), :], lane_roll(packed, 64)
            )
            stage[r, pl.ds(8, 8), pl.ds(256, 128)] = jnp.where(
                low, lane_roll(ab[0][X, col(0), :], 64), packed
            )

    def clear(j):
        def body(i, carry):
            X = REACH + i
            for h in range(3):
                land[X, pl.ds(8 * j, 8), pl.ds(128 * h, 128)] = jnp.zeros((8, 128), f32)
            return carry

        lax.fori_loop(0, rows, body, 0)

    pl.when(c == 0)(lambda: clear(0))
    pl.when(c == n_cross - 1)(lambda: clear(3))

    def margins(X, carry):
        for b in range(2):
            for h in range(2):
                for j in (-1, 4):
                    ub[b][h, X, col(j), :] = jnp.zeros((8, 128), f32)
                    kb[b][h, X, col(j), :] = jnp.zeros((8, 128), f32)
        return carry

    lax.fori_loop(0, rows + 2 * REACH, margins, 0)

    def arrive(ds, dc):
        guarded(dc, halo_copy(-ds, -dc).wait_recv)

    pl.semaphore_wait(barrier, 3 + jnp.where(c > 0, 1, 0) + jnp.where(c < n_cross - 1, 1, 0))
    for dc in (-1, 1):
        guarded(dc, halo_copy(0, dc).start)
    own.wait()

    def out_copy(part):
        return pltpu.make_async_remote_copy(
            src_ref=stage.at[pl.ds(4 * part, 4)],
            dst_ref=o_ref.at[pl.ds(4 * part, 4)],
            send_sem=out_sems.at[part],
            recv_sem=got_sems.at[part],
            device_id=target,
            device_id_type=MESH,
        )

    def finish(part, first, slope):
        init_rows(first, 4)
        flank(first, slope)
        unpack(4 * part, 4)
        out_copy(part).start()

    def mid_copies(side):
        to = peer(2 * side - 1, 0)
        return [
            pltpu.make_async_remote_copy(
                src_ref=src.at[side],
                dst_ref=dst.at[1 - side],
                send_sem=mid_send_sems.at[2 * side + n],
                recv_sem=mid_recv_sems.at[2 * side + n],
                device_id=to,
                device_id_type=MESH,
            )
            for n, (src, dst) in enumerate(((send_u, land_u), (send_a, land_a)))
        ]

    def give(side):
        for i in range(REACH):
            X = REACH + i + side * (rows - REACH)
            for j in range(4):
                for h in range(2):
                    send_u[side, h, i, pl.ds(8 * j, 8), :] = ub[0][h, X, col(j), :]
            for g in range(2):
                send_a[side, i, pl.ds(8 * g, 8), :] = ab[0][X, col(g), :]
        for copy in mid_copies(side):
            copy.start()

    def take(side):
        for copy in mid_copies(1 - side):
            copy.wait_recv()

        for i in range(REACH):
            X = i + side * (rows + REACH)
            u0 = []
            for j in range(4):
                u = [land_u[side, h, i, pl.ds(8 * j, 8), :] for h in range(2)]
                put_cell(0, X, j, u)
                u0.append(u[0])
            for g in range(2):
                put_acid(0, X, g, land_a[side, i, pl.ds(8 * g, 8), :], u0[g], u0[g + 2])

    def finish(part):
        unpack(4 * part, 4)
        out_copy(part).start()

    for dc in (-1, 1):
        arrive(0, dc)
    for ds in (-1, 1):
        halo_copy(ds, 0).start()
    init_rows(0, rows)
    middle(0)
    arrive(-1, 0)
    init_rows(-REACH, REACH)
    flank(0, -REACH, 1)
    give(0)
    arrive(1, 0)
    init_rows(rows, REACH)
    flank(0, rows, -1)
    give(1)
    middle(REACH)
    finish(1)
    finish(2)
    take(0)
    flank(REACH, -4, 1)
    finish(0)
    take(1)
    flank(REACH, rows, -1)
    finish(3)
    for part in range(4):
        out_copy(part).wait()
    for side in range(2):
        for copy in mid_copies(side):
            copy.wait_send()
    for ds, dc in sides:
        guarded(dc, halo_copy(ds, dc).wait_send)


def shards(wafer_state, layer_heat_coefficients, beam_profile, beam_start, beam_steps):
    smem = pl.BlockSpec(memory_space=pltpu.SMEM)
    f32 = jnp.float32
    rows, cols, chans = wafer_state.shape
    X = rows + 2 * REACH
    Y = cols + 2 * HALO
    return pl.pallas_call(
        kernel,
        out_shape=jax.ShapeDtypeStruct(wafer_state.shape, f32),
        in_specs=[smem, smem, smem, pl.BlockSpec(memory_space=pltpu.VMEM), pl.BlockSpec(memory_space=pl.ANY)],
        out_specs=pl.BlockSpec(memory_space=pl.ANY),
        scratch_shapes=[
            pltpu.VMEM((X, Y, chans), f32),
            pltpu.VMEM((rows, cols, chans), f32),
            pltpu.VMEM((2, 2, REACH, Y, 128), f32),
            pltpu.VMEM((2, REACH, 16, 128), f32),
            pltpu.VMEM((2, 2, REACH, Y, 128), f32),
            pltpu.VMEM((2, REACH, 16, 128), f32),
            pltpu.VMEM((2, X, Y + 2 * PAD, 128), f32),
            pltpu.VMEM((2, X, Y + 2 * PAD, 128), f32),
            pltpu.VMEM((2, X, Y + 2 * PAD, 128), f32),
            pltpu.VMEM((2, X, Y + 2 * PAD, 128), f32),
            pltpu.VMEM((X, 16 + 2 * PAD, 128), f32),
            pltpu.VMEM((X, 16 + 2 * PAD, 128), f32),
            pltpu.VMEM((X, 16 + 2 * PAD, 128), f32),
            pltpu.VMEM((X, 16 + 2 * PAD, 128), f32),
            pltpu.VMEM((X, 8, 128), f32),
            pltpu.VMEM((LEVELS * 24, 128), f32),
            pltpu.VMEM((2, Y, 128), f32),
            pltpu.SemaphoreType.DMA((4,)),
            pltpu.SemaphoreType.DMA((4,)),
            pltpu.SemaphoreType.DMA,
            pltpu.SemaphoreType.DMA((4,)),
            pltpu.SemaphoreType.DMA((4,)),
            pltpu.SemaphoreType.DMA((4,)),
            pltpu.SemaphoreType.DMA((4,)),
        ],
        compiler_params=pltpu.CompilerParams(collective_id=0, has_side_effects=True),
    )(beam_profile, beam_start, beam_steps, layer_heat_coefficients, wafer_state)


def solution(mesh):
    in_specs = (P("scan", "cross", None), P(), P(), P(), P())
    out_specs = P("scan", "cross", None)
    return jax.shard_map(shards, mesh=mesh, in_specs=in_specs, out_specs=out_specs, check_vma=False)
```

```python
import jax
import jax.numpy as jnp
from jax import lax
from jax.experimental import pallas as pl
from jax.experimental.pallas import tpu as pltpu
from jax.sharding import PartitionSpec as P

STEPS = 4
SUBSTEPS = 2
LEVELS = STEPS * SUBSTEPS
HALO = LEVELS
REACH = LEVELS // 2
PAD = 8
LOG2E = 1.4426950408889634
MESH = pl.DeviceIdType.MESH

heat_power = 0.5
absorb_depth = 6.0
barrier_energy = 3.0
frequency_multiplier = 0.6
proton_mobility = 0.15


def lane_roll(v, shift):
    return pltpu.roll(v, shift % v.shape[1], axis=1)


def kernel(
    profile_ref, start_ref, steps_ref, coef_ref, x_ref, o_ref,
    land, stage, send_u, send_a, land_u, land_a, ub0, ub1, kb0, kb1, ab0, ab1, db0, db1, pb, spot, pa, send_sems, recv_sems, own_sem, out_sems, got_sems,
    mid_send_sems, mid_recv_sems,
):
    s = lax.axis_index("scan")
    c = lax.axis_index("cross")
    n_scan = lax.axis_size("scan")
    n_cross = lax.axis_size("cross")
    rows = x_ref.shape[0]
    cols = x_ref.shape[1]
    total_x = rows * n_scan
    target = (lax.rem(s + n_scan - STEPS, n_scan), c)
    source = (lax.rem(s + STEPS, n_scan), c)
    f32 = jnp.float32
    ub, kb, ab, db = (ub0, ub1), (kb0, kb1), (ab0, ab1), (db0, db1)

    barrier = pltpu.get_barrier_semaphore()
    sides = [(0, -1), (0, 1), (-1, 0), (1, 0)]

    def peer(ds, dc):
        return (lax.rem(s + ds + n_scan, n_scan), c + dc)

    def exists(dc):
        if dc < 0:
            return c > 0
        if dc > 0:
            return c < n_cross - 1
        return None

    def guarded(dc, fn):
        cond = exists(dc)
        if cond is None:
            fn()
        else:
            pl.when(cond)(fn)

    for ds, dc in sides:
        def greet(ds=ds, dc=dc):
            pl.semaphore_signal(barrier, 1, device_id=peer(ds, dc), device_id_type=MESH)
        guarded(dc, greet)
    pl.semaphore_signal(barrier, 1, device_id=target, device_id_type=MESH)

    own = pltpu.make_async_copy(
        x_ref, land.at[pl.ds(REACH, rows), pl.ds(HALO, cols), :], own_sem
    )
    own.start()

    def span(d, length, sending, halo):
        if d == 0:
            return pl.ds(0 if sending else halo, length)
        if d > 0:
            return pl.ds(length - halo if sending else 0, halo)
        return pl.ds(0 if sending else halo + length, halo)

    def halo_copy(ds, dc, part=0):
        if ds == 0:
            k = sides.index((ds, dc))
            source_ref = x_ref.at[:, span(dc, cols, True, HALO), :]
            landing = land.at[pl.ds(REACH, rows), span(dc, cols, False, HALO), :]
        else:
            k = (2 if ds < 0 else 5) + part
            if part == 0:
                places = pl.ds(HALO, cols)
                source_ref = x_ref.at[span(ds, rows, True, REACH)]
            else:
                places = pl.ds(0 if part == 1 else HALO + cols, HALO)
                source_ref = land.at[pl.ds(REACH if ds < 0 else rows, REACH), places, :]
            landing = land.at[span(ds, rows, False, REACH), places, :]
        return pltpu.make_async_remote_copy(
            src_ref=source_ref,
            dst_ref=landing,
            send_sem=send_sems.at[k],
            recv_sem=recv_sems.at[k],
            device_id=peer(ds, dc),
            device_id_type=MESH,
        )

    lane = lax.broadcasted_iota(jnp.int32, (8, 128), 1)
    sub = lax.broadcasted_iota(jnp.int32, (8, 128), 0)
    low = lane < 64
    last_lane = lane == 127
    first_lane = lane == 0
    half_coef = [
        jnp.broadcast_to((0.5 * coef_ref[pl.ds(128 * h, 128)])[None, :], (8, 128)) for h in range(2)
    ]
    floor_coef = half_coef[1]

    for t in range(1, LEVELS + 1):
        f = (t - 1) // SUBSTEPS
        n = (t - 1) % SUBSTEPS
        center = (start_ref[f] + n * steps_ref[f]).astype(f32)
        for g in range(3):
            at = sub + (8 * g - REACH) + (s * rows - rows * f + 2 * total_x)
            where_x = lax.rem(at, jnp.int32(total_x)).astype(f32)
            ratio = (where_x - center) * (1.0 / float(rows // 2))
            spot[pl.ds((t - 1) * 24 + 8 * g, 8), :] = jnp.exp(-ratio * ratio)

    z0 = lane.astype(f32)
    absorb = [
        jnp.where(z0 + (128.0 * h) >= 64.0, jnp.exp(-(z0 + (128.0 * h - 64.0)) / absorb_depth), 0.0)
        for h in range(2)
    ]
    for j in range(4):
        shine = jnp.zeros((8, 128), f32)
        for i in range(8):
            place = c * cols - HALO + 8 * j + i
            place = jnp.clip(place, 0, n_cross * cols - 1)
            shine = jnp.where(sub == i, profile_ref[place], shine)
        for h in range(2):
            pa[h, pl.ds(8 * j, 8), :] = (0.5 * heat_power) * shine * absorb[h]

    left_f = jnp.where(c > 0, 1.0, 0.0).astype(f32)
    right_f = jnp.where(c < n_cross - 1, 1.0, 0.0).astype(f32)
    edge_f = [left_f, None, None, right_f]
    edge_a = [jnp.where(low, left_f, 1.0), jnp.where(low, 1.0, right_f)]

    def col(j, dy=0):
        return pl.ds(PAD + 8 * j + dy, 8)

    def put_cell(b, X, j, u):
        for h in range(2):
            ub[b][h, X, col(j), :] = u[h]
            kb[b][h, X, col(j), :] = half_coef[h] * (1.0 / (1.0 + u[h] * u[h]))

    def put_acid(b, X, g, acid, u_low, u_high):
        u = jnp.where(low, u_low, lane_roll(u_high, 64))
        sq = u * u
        d = (0.5 * proton_mobility * sq) * (1.0 / (0.25 + sq))
        ghost = pl.ds(PAD + 16, 8) if g == 0 else pl.ds(0, 8)
        ab[b][X, col(g), :] = acid
        ab[b][X, ghost, :] = lane_roll(acid, 64)
        db[b][X, col(g), :] = d
        db[b][X, ghost, :] = lane_roll(d, 64)

    def init_rows(first, count):
        def body(q, carry):
            for i in range(4):
                X = first + REACH + 4 * q + i
                u0 = []
                for j in range(4):
                    u = [0.5 * land[X, pl.ds(8 * j, 8), pl.ds(128 * h, 128)] for h in range(2)]
                    put_cell(0, X, j, u)
                    u0.append(u[0])
                last = [land[X, pl.ds(8 * j, 8), pl.ds(256, 128)] for j in range(4)]
                for g in range(2):
                    acid = jnp.where(low, last[g], lane_roll(last[g + 2], 64))
                    put_acid(0, X, g, acid, u0[g], u0[g + 2])
                pb[X] = jnp.where(low, lane_roll(last[1], 64), last[2])
            return carry

        lax.fori_loop(0, count // 4, body, 0)

    inner_a = jnp.where(lax.rem(lane, 64) < 63, 1.0, 0.0).astype(f32)

    def block(t, r0, a, b, n, final=False):
        X0 = r0 + REACH
        beams = [
            jnp.broadcast_to(spot[pl.ds((t - 1) * 24 + X0 + i, 1), :], (8, 128)) for i in range(n)
        ]

        def side(vals, facs, i, load_v, load_f):
            cur, fac = vals[i], facs[i]
            flux_up = (fac + load_f(i, 1)) * (load_v(i, 1) - cur)
            flux_dn = (fac + load_f(i, -1)) * (cur - load_v(i, -1))
            return flux_up - flux_dn

        def along(vals, facs):
            flux = [(facs[i] + facs[i + 1]) * (vals[i + 1] - vals[i]) for i in range(-1, n)]
            return [flux[i + 1] - flux[i] for i in range(n)]

        fresh = {}
        for g in range(2):
            for j in tuple(j for j in (g, g + 2) if not final or j in (1, 2)):
                U = [
                    {i: ub[a][h, X0 + i, col(j), :] for i in range(-1, n + 1)} for h in range(2)
                ]
                K = [
                    {i: kb[a][h, X0 + i, col(j), :] for i in range(-1, n + 1)} for h in range(2)
                ]
                xn = [along(U[h], K[h]) for h in range(2)]
                for i in range(n):
                    ur = [lane_roll(U[h][i], -1) for h in range(2)]
                    kr = [lane_roll(K[h][i], -1) for h in range(2)]
                    un = [jnp.where(last_lane, ur[1], ur[0]), jnp.where(last_lane, 0.0, ur[1])]
                    kn = [jnp.where(last_lane, kr[1], kr[0]), jnp.where(last_lane, floor_coef, kr[1])]
                    fz = [(K[h][i] + kn[h]) * (un[h] - U[h][i]) for h in range(2)]
                    fr = [lane_roll(fz[h], 1) for h in range(2)]
                    fp = [jnp.where(first_lane, 0.0, fr[0]), jnp.where(first_lane, fr[0], fr[1])]
                    out = []
                    for h in range(2):
                        yn = side(
                            U[h], K[h], i,
                            lambda i, dy, h=h: ub[a][h, X0 + i, col(j, dy), :],
                            lambda i, dy, h=h: kb[a][h, X0 + i, col(j, dy), :],
                        )
                        value = U[h][i] + ((xn[h][i] + yn) + (fz[h] - fp[h]))
                        value = value + beams[i] * pa[h, pl.ds(8 * j, 8), :]
                        if edge_f[j] is not None:
                            value = value * edge_f[j]
                        out.append(value)
                    if final:
                        for h in range(2):
                            ub[b][h, X0 + i, col(j), :] = out[h]
                        continue
                    put_cell(b, X0 + i, j, out)
                    fresh[j, i] = out[0]
            A = {i: ab[a][X0 + i, col(g), :] for i in range(-1, n + 1)}
            D = {i: db[a][X0 + i, col(g), :] for i in range(-1, n + 1)}
            xa = along(A, D)
            for i in range(n):
                fz = ((D[i] + lane_roll(D[i], -1)) * (lane_roll(A[i], -1) - A[i])) * inner_a
                ya = side(
                    A, D, i,
                    lambda i, dy: ab[a][X0 + i, col(g, dy), :],
                    lambda i, dy: db[a][X0 + i, col(g, dy), :],
                )
                value = A[i] + ((xa[i] + ya) + (fz - lane_roll(fz, 1)))
                value = value * edge_a[g]
                if final:
                    ab[b][X0 + i, col(g), :] = value
                else:
                    put_acid(b, X0 + i, g, value, fresh[g, i], fresh[g + 2, i])

        @pl.when(jnp.logical_and(r0 > -n, r0 < rows))
        def _():
            for i in range(n):
                tp = jnp.where(
                    low, ub[a][0, X0 + i, col(1), :], lane_roll(ub[a][0, X0 + i, col(2), :], 64)
                )
                ap = jnp.where(low, ab[a][X0 + i, col(1), :], ab[a][X0 + i, col(0), :])
                rate = jnp.exp2((-0.5 * barrier_energy * LOG2E) * (1.0 / (0.5 + tp)))
                pb[X0 + i] = pb[X0 + i] * (1.0 - (frequency_multiplier * ap) * rate)

        for i in range(n):
            r = r0 + i
            owner = lax.rem(s + lax.div(r + rows, rows) - 1 + n_scan, n_scan)

            if b == 1:
                continue

            @pl.when(owner == lax.div(t, 2) - 1)
            def _(i=i):
                zero = jnp.zeros((8, 128), f32)
                for j in range(4):
                    for h in range(2):
                        ub[b][h, X0 + i, col(j), :] = zero
                        kb[b][h, X0 + i, col(j), :] = half_coef[h]
                for g in range(4):
                    db[b][X0 + i, pl.ds(8 * g, 8), :] = zero

    def levels_in_pairs(level, base):
        def two(m, carry):
            level(2 * m + 1, base + 2 * m + 1, 0, 1, False)
            level(2 * m + 2, base + 2 * m + 2, 1, 0, False)
            return carry

        lax.fori_loop(0, REACH // 2, two, 0)

    def middle(base, count):
        def level(k, t, a, b, final):
            def four(i, carry):
                block(t, k + 4 * i, a, b, 4, final)
                return carry

            lax.fori_loop(0, lax.div(count - 2 * k, 4), four, 0)
            if b == 1:
                block(t, count - 2 - k, a, b, 2, final)

        levels_in_pairs(level, base)

    def flank(base, first, slope):
        levels_in_pairs(
            lambda k, t, a, b, final: block(t, first + slope * k, a, b, 4, final), base
        )

    def unpack(first, count):
        for i in range(count):
            r = first + i
            X = r + REACH
            packed = pb[X]
            for j in (1, 2):
                for h in range(2):
                    stage[r, pl.ds(8 * j - 8, 8), pl.ds(128 * h, 128)] = 2.0 * ub[0][h, X, col(j), :]
            stage[r, pl.ds(0, 8), pl.ds(256, 128)] = jnp.where(
                low, ab[0][X, col(1), :], lane_roll(packed, 64)
            )
            stage[r, pl.ds(8, 8), pl.ds(256, 128)] = jnp.where(
                low, lane_roll(ab[0][X, col(0), :], 64), packed
            )

    def clear(j):
        def body(i, carry):
            X = REACH + i
            for h in range(3):
                land[X, pl.ds(8 * j, 8), pl.ds(128 * h, 128)] = jnp.zeros((8, 128), f32)
            return carry

        lax.fori_loop(0, rows, body, 0)

    pl.when(c == 0)(lambda: clear(0))
    pl.when(c == n_cross - 1)(lambda: clear(3))

    def margins(X, carry):
        for b in range(2):
            for h in range(2):
                for j in (-1, 4):
                    ub[b][h, X, col(j), :] = jnp.zeros((8, 128), f32)
                    kb[b][h, X, col(j), :] = jnp.zeros((8, 128), f32)
        return carry

    lax.fori_loop(0, rows + 2 * REACH, margins, 0)

    def arrive(ds, dc):
        for part in range(3 if dc == 0 else 1):
            guarded(dc, halo_copy(-ds, -dc, part).wait_recv)

    pl.semaphore_wait(barrier, 3 + jnp.where(c > 0, 1, 0) + jnp.where(c < n_cross - 1, 1, 0))
    for dc in (-1, 1):
        guarded(dc, halo_copy(0, dc).start)
    for ds in (-1, 1):
        halo_copy(ds, 0).start()
    own.wait()

    def out_copy(part):
        return pltpu.make_async_remote_copy(
            src_ref=stage.at[pl.ds(4 * part, 4)],
            dst_ref=o_ref.at[pl.ds(4 * part, 4)],
            send_sem=out_sems.at[part],
            recv_sem=got_sems.at[part],
            device_id=target,
            device_id_type=MESH,
        )

    def finish(part, first, slope):
        init_rows(first, 4)
        flank(first, slope)
        unpack(4 * part, 4)
        out_copy(part).start()

    def mid_copies(side):
        to = peer(2 * side - 1, 0)
        return [
            pltpu.make_async_remote_copy(
                src_ref=src.at[side],
                dst_ref=dst.at[1 - side],
                send_sem=mid_send_sems.at[2 * side + n],
                recv_sem=mid_recv_sems.at[2 * side + n],
                device_id=to,
                device_id_type=MESH,
            )
            for n, (src, dst) in enumerate(((send_u, land_u), (send_a, land_a)))
        ]

    def give(side):
        for i in range(REACH):
            X = REACH + i + side * (rows - REACH)
            for j in range(4):
                for h in range(2):
                    send_u[side, h, i, pl.ds(8 * j, 8), :] = ub[0][h, X, col(j), :]
            for g in range(2):
                send_a[side, i, pl.ds(8 * g, 8), :] = ab[0][X, col(g), :]
        for copy in mid_copies(side):
            copy.start()

    def take(side):
        for copy in mid_copies(1 - side):
            copy.wait_recv()

        for i in range(REACH):
            X = i + side * (rows + REACH)
            u0 = []
            for j in range(4):
                u = [land_u[side, h, i, pl.ds(8 * j, 8), :] for h in range(2)]
                put_cell(0, X, j, u)
                u0.append(u[0])
            for g in range(2):
                put_acid(0, X, g, land_a[side, i, pl.ds(8 * g, 8), :], u0[g], u0[g + 2])

    def finish(part):
        unpack(4 * part, 4)
        out_copy(part).start()

    for dc in (-1, 1):
        arrive(0, dc)
    for ds in (-1, 1):
        for part in (1, 2):
            halo_copy(ds, 0, part).start()
    init_rows(0, rows)
    middle(0, rows)
    arrive(-1, 0)
    init_rows(-REACH, REACH)
    flank(0, -REACH, 1)
    give(0)
    arrive(1, 0)
    init_rows(rows, REACH)
    flank(0, rows, -1)
    give(1)
    middle(REACH, rows - 4)
    finish(1)

    def closing(n, carry):
        pl.when(n == 1)(lambda: take(1))
        pl.when(n == 2)(lambda: take(0))
        first = jnp.where(n == 0, rows - 4, jnp.where(n == 1, rows, -REACH))
        slope = jnp.where(n == 2, 1, -1)
        flank(REACH, first, slope)
        finish(jnp.where(n == 0, 2, jnp.where(n == 1, 3, 0)))
        return carry

    lax.fori_loop(0, 3, closing, 0)
    for part in range(4):
        out_copy(part).wait()
    for side in range(2):
        for copy in mid_copies(side):
            copy.wait_send()
    for ds, dc in sides:
        for part in range(3 if dc == 0 else 1):
            guarded(dc, halo_copy(ds, dc, part).wait_send)


def shards(wafer_state, layer_heat_coefficients, beam_profile, beam_start, beam_steps):
    smem = pl.BlockSpec(memory_space=pltpu.SMEM)
    f32 = jnp.float32
    rows, cols, chans = wafer_state.shape
    X = rows + 2 * REACH
    Y = cols + 2 * HALO
    return pl.pallas_call(
        kernel,
        out_shape=jax.ShapeDtypeStruct(wafer_state.shape, f32),
        in_specs=[smem, smem, smem, pl.BlockSpec(memory_space=pltpu.VMEM), pl.BlockSpec(memory_space=pl.ANY)],
        out_specs=pl.BlockSpec(memory_space=pl.ANY),
        scratch_shapes=[
            pltpu.VMEM((X, Y, chans), f32),
            pltpu.VMEM((rows, cols, chans), f32),
            pltpu.VMEM((2, 2, REACH, Y, 128), f32),
            pltpu.VMEM((2, REACH, 16, 128), f32),
            pltpu.VMEM((2, 2, REACH, Y, 128), f32),
            pltpu.VMEM((2, REACH, 16, 128), f32),
            pltpu.VMEM((2, X, Y + 2 * PAD, 128), f32),
            pltpu.VMEM((2, X, Y + 2 * PAD, 128), f32),
            pltpu.VMEM((2, X, Y + 2 * PAD, 128), f32),
            pltpu.VMEM((2, X, Y + 2 * PAD, 128), f32),
            pltpu.VMEM((X, 16 + 2 * PAD, 128), f32),
            pltpu.VMEM((X, 16 + 2 * PAD, 128), f32),
            pltpu.VMEM((X, 16 + 2 * PAD, 128), f32),
            pltpu.VMEM((X, 16 + 2 * PAD, 128), f32),
            pltpu.VMEM((X, 8, 128), f32),
            pltpu.VMEM((LEVELS * 24, 128), f32),
            pltpu.VMEM((2, Y, 128), f32),
            pltpu.SemaphoreType.DMA((8,)),
            pltpu.SemaphoreType.DMA((8,)),
            pltpu.SemaphoreType.DMA,
            pltpu.SemaphoreType.DMA((4,)),
            pltpu.SemaphoreType.DMA((4,)),
            pltpu.SemaphoreType.DMA((4,)),
            pltpu.SemaphoreType.DMA((4,)),
        ],
        compiler_params=pltpu.CompilerParams(collective_id=0, has_side_effects=True),
    )(beam_profile, beam_start, beam_steps, layer_heat_coefficients, wafer_state)


def solution(mesh):
    in_specs = (P("scan", "cross", None), P(), P(), P(), P())
    out_specs = P("scan", "cross", None)
    return jax.shard_map(shards, mesh=mesh, in_specs=in_specs, out_specs=out_specs, check_vma=False)
```

```python
import jax
import jax.numpy as jnp
from jax import lax
from jax.experimental import pallas as pl
from jax.experimental.pallas import tpu as pltpu
from jax.sharding import PartitionSpec as P

STEPS = 4
SUBSTEPS = 2
LEVELS = STEPS * SUBSTEPS
HALO = LEVELS
REACH = LEVELS // 2
PAD = 8
LOG2E = 1.4426950408889634
MESH = pl.DeviceIdType.MESH

heat_power = 0.5
absorb_depth = 6.0
barrier_energy = 3.0
frequency_multiplier = 0.6
proton_mobility = 0.15


def lane_roll(v, shift):
    return pltpu.roll(v, shift % v.shape[1], axis=1)


def kernel(
    profile_ref, start_ref, steps_ref, coef_ref, x_ref, o_ref,
    land, stage, send_u, send_a, land_u, land_a, ub0, ub1, kb0, kb1, ab0, ab1, db0, db1, pb, spot, pa, send_sems, recv_sems, own_sem, out_sems, got_sems,
    mid_send_sems, mid_recv_sems,
):
    s = lax.axis_index("scan")
    c = lax.axis_index("cross")
    n_scan = lax.axis_size("scan")
    n_cross = lax.axis_size("cross")
    rows = x_ref.shape[0]
    cols = x_ref.shape[1]
    total_x = rows * n_scan
    target = (lax.rem(s + n_scan - STEPS, n_scan), c)
    source = (lax.rem(s + STEPS, n_scan), c)
    f32 = jnp.float32
    ub, kb, ab, db = (ub0, ub1), (kb0, kb1), (ab0, ab1), (db0, db1)

    barrier = pltpu.get_barrier_semaphore()
    sides = [(0, -1), (0, 1), (-1, 0), (1, 0)]

    def peer(ds, dc):
        return (lax.rem(s + ds + n_scan, n_scan), c + dc)

    def exists(dc):
        if dc < 0:
            return c > 0
        if dc > 0:
            return c < n_cross - 1
        return None

    def guarded(dc, fn):
        cond = exists(dc)
        if cond is None:
            fn()
        else:
            pl.when(cond)(fn)

    for ds, dc in sides:
        def greet(ds=ds, dc=dc):
            pl.semaphore_signal(barrier, 1, device_id=peer(ds, dc), device_id_type=MESH)
        guarded(dc, greet)
    pl.semaphore_signal(barrier, 1, device_id=target, device_id_type=MESH)

    own = pltpu.make_async_copy(
        x_ref, land.at[pl.ds(REACH, rows), pl.ds(HALO, cols), :], own_sem
    )
    own.start()

    def span(d, length, sending, halo):
        if d == 0:
            return pl.ds(0 if sending else halo, length)
        if d > 0:
            return pl.ds(length - halo if sending else 0, halo)
        return pl.ds(0 if sending else halo + length, halo)

    def halo_copy(ds, dc, part=0):
        if ds == 0:
            k = sides.index((ds, dc)) + 8 * part
            half = rows // 2
            source_ref = x_ref.at[pl.ds(half * part, half), span(dc, cols, True, HALO), :]
            landing = land.at[pl.ds(REACH + half * part, half), span(dc, cols, False, HALO), :]
        else:
            k = (2 if ds < 0 else 5) + part
            if part == 0:
                places = pl.ds(HALO, cols)
                source_ref = x_ref.at[span(ds, rows, True, REACH)]
            else:
                places = pl.ds(0 if part == 1 else HALO + cols, HALO)
                source_ref = land.at[pl.ds(REACH if ds < 0 else rows, REACH), places, :]
            landing = land.at[span(ds, rows, False, REACH), places, :]
        return pltpu.make_async_remote_copy(
            src_ref=source_ref,
            dst_ref=landing,
            send_sem=send_sems.at[k],
            recv_sem=recv_sems.at[k],
            device_id=peer(ds, dc),
            device_id_type=MESH,
        )

    lane = lax.broadcasted_iota(jnp.int32, (8, 128), 1)
    sub = lax.broadcasted_iota(jnp.int32, (8, 128), 0)
    low = lane < 64
    last_lane = lane == 127
    first_lane = lane == 0
    half_coef = [
        jnp.broadcast_to((0.5 * coef_ref[pl.ds(128 * h, 128)])[None, :], (8, 128)) for h in range(2)
    ]
    floor_coef = half_coef[1]

    for t in range(1, LEVELS + 1):
        f = (t - 1) // SUBSTEPS
        n = (t - 1) % SUBSTEPS
        center = (start_ref[f] + n * steps_ref[f]).astype(f32)
        for g in range(3):
            at = sub + (8 * g - REACH) + (s * rows - rows * f + 2 * total_x)
            where_x = lax.rem(at, jnp.int32(total_x)).astype(f32)
            ratio = (where_x - center) * (1.0 / float(rows // 2))
            spot[pl.ds((t - 1) * 24 + 8 * g, 8), :] = jnp.exp(-ratio * ratio)

    z0 = lane.astype(f32)
    absorb = [
        jnp.where(z0 + (128.0 * h) >= 64.0, jnp.exp(-(z0 + (128.0 * h - 64.0)) / absorb_depth), 0.0)
        for h in range(2)
    ]
    for j in range(4):
        shine = jnp.zeros((8, 128), f32)
        for i in range(8):
            place = c * cols - HALO + 8 * j + i
            place = jnp.clip(place, 0, n_cross * cols - 1)
            shine = jnp.where(sub == i, profile_ref[place], shine)
        for h in range(2):
            pa[h, pl.ds(8 * j, 8), :] = (0.5 * heat_power) * shine * absorb[h]

    left_f = jnp.where(c > 0, 1.0, 0.0).astype(f32)
    right_f = jnp.where(c < n_cross - 1, 1.0, 0.0).astype(f32)
    edge_f = [left_f, None, None, right_f]
    edge_a = [jnp.where(low, left_f, 1.0), jnp.where(low, 1.0, right_f)]

    def col(j, dy=0):
        return pl.ds(PAD + 8 * j + dy, 8)

    def put_cell(b, X, j, u):
        for h in range(2):
            ub[b][h, X, col(j), :] = u[h]
            kb[b][h, X, col(j), :] = half_coef[h] * (1.0 / (1.0 + u[h] * u[h]))

    def put_acid(b, X, g, acid, u_low, u_high):
        u = jnp.where(low, u_low, lane_roll(u_high, 64))
        sq = u * u
        d = (0.5 * proton_mobility * sq) * (1.0 / (0.25 + sq))
        ghost = pl.ds(PAD + 16, 8) if g == 0 else pl.ds(0, 8)
        ab[b][X, col(g), :] = acid
        ab[b][X, ghost, :] = lane_roll(acid, 64)
        db[b][X, col(g), :] = d
        db[b][X, ghost, :] = lane_roll(d, 64)

    def init_rows(first, count):
        def body(q, carry):
            for i in range(4):
                X = first + REACH + 4 * q + i
                u0 = []
                for j in range(4):
                    u = [0.5 * land[X, pl.ds(8 * j, 8), pl.ds(128 * h, 128)] for h in range(2)]
                    put_cell(0, X, j, u)
                    u0.append(u[0])
                last = [land[X, pl.ds(8 * j, 8), pl.ds(256, 128)] for j in range(4)]
                for g in range(2):
                    acid = jnp.where(low, last[g], lane_roll(last[g + 2], 64))
                    put_acid(0, X, g, acid, u0[g], u0[g + 2])
                pb[X] = jnp.where(low, lane_roll(last[1], 64), last[2])
            return carry

        lax.fori_loop(0, count // 4, body, 0)

    inner_a = jnp.where(lax.rem(lane, 64) < 63, 1.0, 0.0).astype(f32)

    def block(t, r0, a, b, n, final=False):
        X0 = r0 + REACH
        beams = [
            jnp.broadcast_to(spot[pl.ds((t - 1) * 24 + X0 + i, 1), :], (8, 128)) for i in range(n)
        ]

        def side(vals, facs, i, load_v, load_f):
            cur, fac = vals[i], facs[i]
            flux_up = (fac + load_f(i, 1)) * (load_v(i, 1) - cur)
            flux_dn = (fac + load_f(i, -1)) * (cur - load_v(i, -1))
            return flux_up - flux_dn

        def along(vals, facs):
            flux = [(facs[i] + facs[i + 1]) * (vals[i + 1] - vals[i]) for i in range(-1, n)]
            return [flux[i + 1] - flux[i] for i in range(n)]

        fresh = {}
        for g in range(2):
            for j in tuple(j for j in (g, g + 2) if not final or j in (1, 2)):
                U = [
                    {i: ub[a][h, X0 + i, col(j), :] for i in range(-1, n + 1)} for h in range(2)
                ]
                K = [
                    {i: kb[a][h, X0 + i, col(j), :] for i in range(-1, n + 1)} for h in range(2)
                ]
                xn = [along(U[h], K[h]) for h in range(2)]
                for i in range(n):
                    ur = [lane_roll(U[h][i], -1) for h in range(2)]
                    kr = [lane_roll(K[h][i], -1) for h in range(2)]
                    un = [jnp.where(last_lane, ur[1], ur[0]), jnp.where(last_lane, 0.0, ur[1])]
                    kn = [jnp.where(last_lane, kr[1], kr[0]), jnp.where(last_lane, floor_coef, kr[1])]
                    fz = [(K[h][i] + kn[h]) * (un[h] - U[h][i]) for h in range(2)]
                    fr = [lane_roll(fz[h], 1) for h in range(2)]
                    fp = [jnp.where(first_lane, 0.0, fr[0]), jnp.where(first_lane, fr[0], fr[1])]
                    out = []
                    for h in range(2):
                        yn = side(
                            U[h], K[h], i,
                            lambda i, dy, h=h: ub[a][h, X0 + i, col(j, dy), :],
                            lambda i, dy, h=h: kb[a][h, X0 + i, col(j, dy), :],
                        )
                        value = U[h][i] + ((xn[h][i] + yn) + (fz[h] - fp[h]))
                        value = value + beams[i] * pa[h, pl.ds(8 * j, 8), :]
                        if edge_f[j] is not None:
                            value = value * edge_f[j]
                        out.append(value)
                    if final:
                        for h in range(2):
                            ub[b][h, X0 + i, col(j), :] = out[h]
                        continue
                    put_cell(b, X0 + i, j, out)
                    fresh[j, i] = out[0]
            A = {i: ab[a][X0 + i, col(g), :] for i in range(-1, n + 1)}
            D = {i: db[a][X0 + i, col(g), :] for i in range(-1, n + 1)}
            xa = along(A, D)
            for i in range(n):
                fz = ((D[i] + lane_roll(D[i], -1)) * (lane_roll(A[i], -1) - A[i])) * inner_a
                ya = side(
                    A, D, i,
                    lambda i, dy: ab[a][X0 + i, col(g, dy), :],
                    lambda i, dy: db[a][X0 + i, col(g, dy), :],
                )
                value = A[i] + ((xa[i] + ya) + (fz - lane_roll(fz, 1)))
                value = value * edge_a[g]
                if final:
                    ab[b][X0 + i, col(g), :] = value
                else:
                    put_acid(b, X0 + i, g, value, fresh[g, i], fresh[g + 2, i])

        @pl.when(jnp.logical_and(r0 > -n, r0 < rows))
        def _():
            for i in range(n):
                tp = jnp.where(
                    low, ub[a][0, X0 + i, col(1), :], lane_roll(ub[a][0, X0 + i, col(2), :], 64)
                )
                ap = jnp.where(low, ab[a][X0 + i, col(1), :], ab[a][X0 + i, col(0), :])
                rate = jnp.exp2((-0.5 * barrier_energy * LOG2E) * (1.0 / (0.5 + tp)))
                pb[X0 + i] = pb[X0 + i] * (1.0 - (frequency_multiplier * ap) * rate)

        for i in range(n):
            r = r0 + i
            owner = lax.rem(s + lax.div(r + rows, rows) - 1 + n_scan, n_scan)

            if b == 1:
                continue

            @pl.when(owner == lax.div(t, 2) - 1)
            def _(i=i):
                zero = jnp.zeros((8, 128), f32)
                for j in range(4):
                    for h in range(2):
                        ub[b][h, X0 + i, col(j), :] = zero
                        kb[b][h, X0 + i, col(j), :] = half_coef[h]
                for g in range(4):
                    db[b][X0 + i, pl.ds(8 * g, 8), :] = zero

    def levels_in_pairs(level, base):
        def two(m, carry):
            level(2 * m + 1, base + 2 * m + 1, 0, 1, False)
            level(2 * m + 2, base + 2 * m + 2, 1, 0, False)
            return carry

        lax.fori_loop(0, REACH // 2, two, 0)

    def middle(base, count):
        def level(k, t, a, b, final):
            def four(i, carry):
                block(t, k + 4 * i, a, b, 4, final)
                return carry

            lax.fori_loop(0, lax.div(count - 2 * k, 4), four, 0)
            if b == 1:
                block(t, count - 2 - k, a, b, 2, final)

        levels_in_pairs(level, base)

    def flank(base, first, slope):
        levels_in_pairs(
            lambda k, t, a, b, final: block(t, first + slope * k, a, b, 4, final), base
        )

    def unpack(first, count):
        for i in range(count):
            r = first + i
            X = r + REACH
            packed = pb[X]
            for j in (1, 2):
                for h in range(2):
                    stage[r, pl.ds(8 * j - 8, 8), pl.ds(128 * h, 128)] = 2.0 * ub[0][h, X, col(j), :]
            stage[r, pl.ds(0, 8), pl.ds(256, 128)] = jnp.where(
                low, ab[0][X, col(1), :], lane_roll(packed, 64)
            )
            stage[r, pl.ds(8, 8), pl.ds(256, 128)] = jnp.where(
                low, lane_roll(ab[0][X, col(0), :], 64), packed
            )

    def clear(j):
        def body(i, carry):
            X = REACH + i
            for h in range(3):
                land[X, pl.ds(8 * j, 8), pl.ds(128 * h, 128)] = jnp.zeros((8, 128), f32)
            return carry

        lax.fori_loop(0, rows, body, 0)

    pl.when(c == 0)(lambda: clear(0))
    pl.when(c == n_cross - 1)(lambda: clear(3))

    def margins(X, carry):
        for b in range(2):
            for h in range(2):
                for j in (-1, 4):
                    ub[b][h, X, col(j), :] = jnp.zeros((8, 128), f32)
                    kb[b][h, X, col(j), :] = jnp.zeros((8, 128), f32)
        return carry

    lax.fori_loop(0, rows + 2 * REACH, margins, 0)

    def arrive(ds, dc, parts=(0, 1, 2)):
        for part in parts:
            guarded(dc, halo_copy(-ds, -dc, part).wait_recv)

    pl.semaphore_wait(barrier, 3 + jnp.where(c > 0, 1, 0) + jnp.where(c < n_cross - 1, 1, 0))
    for part in range(2):
        for dc in (-1, 1):
            guarded(dc, halo_copy(0, dc, part).start)
    for ds in (-1, 1):
        halo_copy(ds, 0).start()
    own.wait()

    def out_copy(part):
        return pltpu.make_async_remote_copy(
            src_ref=stage.at[pl.ds(4 * part, 4)],
            dst_ref=o_ref.at[pl.ds(4 * part, 4)],
            send_sem=out_sems.at[part],
            recv_sem=got_sems.at[part],
            device_id=target,
            device_id_type=MESH,
        )

    def finish(part, first, slope):
        init_rows(first, 4)
        flank(first, slope)
        unpack(4 * part, 4)
        out_copy(part).start()

    def mid_copies(side):
        to = peer(2 * side - 1, 0)
        return [
            pltpu.make_async_remote_copy(
                src_ref=src.at[side],
                dst_ref=dst.at[1 - side],
                send_sem=mid_send_sems.at[2 * side + n],
                recv_sem=mid_recv_sems.at[2 * side + n],
                device_id=to,
                device_id_type=MESH,
            )
            for n, (src, dst) in enumerate(((send_u, land_u), (send_a, land_a)))
        ]

    def give(side):
        for i in range(REACH):
            X = REACH + i + side * (rows - REACH)
            for j in range(4):
                for h in range(2):
                    send_u[side, h, i, pl.ds(8 * j, 8), :] = ub[0][h, X, col(j), :]
            for g in range(2):
                send_a[side, i, pl.ds(8 * g, 8), :] = ab[0][X, col(g), :]
        for copy in mid_copies(side):
            copy.start()

    def take(side):
        for copy in mid_copies(1 - side):
            copy.wait_recv()

        for i in range(REACH):
            X = i + side * (rows + REACH)
            u0 = []
            for j in range(4):
                u = [land_u[side, h, i, pl.ds(8 * j, 8), :] for h in range(2)]
                put_cell(0, X, j, u)
                u0.append(u[0])
            for g in range(2):
                put_acid(0, X, g, land_a[side, i, pl.ds(8 * g, 8), :], u0[g], u0[g + 2])

    def finish(part):
        unpack(4 * part, 4)
        out_copy(part).start()

    for n, ds in enumerate((-1, 1)):
        for dc in (-1, 1):
            arrive(0, dc, (n,))
        for part in (1, 2):
            halo_copy(ds, 0, part).start()
        init_rows(n * (rows // 2), rows // 2)
    middle(0, rows)

    def opening(n, carry):
        pl.when(n == 0)(lambda: arrive(-1, 0))
        pl.when(n == 1)(lambda: arrive(1, 0))
        first = jnp.where(n == 0, -REACH, rows)
        init_rows(first, REACH)
        flank(0, first, jnp.where(n == 0, 1, -1))
        pl.when(n == 0)(lambda: give(0))
        pl.when(n == 1)(lambda: give(1))
        return carry

    lax.fori_loop(0, 2, opening, 0)
    middle(REACH, rows - 4)
    finish(1)

    def closing(n, carry):
        pl.when(n == 1)(lambda: take(1))
        pl.when(n == 2)(lambda: take(0))
        first = jnp.where(n == 0, rows - 4, jnp.where(n == 1, rows, -REACH))
        slope = jnp.where(n == 2, 1, -1)
        flank(REACH, first, slope)
        finish(jnp.where(n == 0, 2, jnp.where(n == 1, 3, 0)))
        return carry

    lax.fori_loop(0, 3, closing, 0)
    for part in range(4):
        out_copy(part).wait()
    for side in range(2):
        for copy in mid_copies(side):
            copy.wait_send()
    for ds, dc in sides:
        for part in range(3 if dc == 0 else 2):
            guarded(dc, halo_copy(ds, dc, part).wait_send)


def shards(wafer_state, layer_heat_coefficients, beam_profile, beam_start, beam_steps):
    smem = pl.BlockSpec(memory_space=pltpu.SMEM)
    f32 = jnp.float32
    rows, cols, chans = wafer_state.shape
    X = rows + 2 * REACH
    Y = cols + 2 * HALO
    return pl.pallas_call(
        kernel,
        out_shape=jax.ShapeDtypeStruct(wafer_state.shape, f32),
        in_specs=[smem, smem, smem, pl.BlockSpec(memory_space=pltpu.VMEM), pl.BlockSpec(memory_space=pl.ANY)],
        out_specs=pl.BlockSpec(memory_space=pl.ANY),
        scratch_shapes=[
            pltpu.VMEM((X, Y, chans), f32),
            pltpu.VMEM((rows, cols, chans), f32),
            pltpu.VMEM((2, 2, REACH, Y, 128), f32),
            pltpu.VMEM((2, REACH, 16, 128), f32),
            pltpu.VMEM((2, 2, REACH, Y, 128), f32),
            pltpu.VMEM((2, REACH, 16, 128), f32),
            pltpu.VMEM((2, X, Y + 2 * PAD, 128), f32),
            pltpu.VMEM((2, X, Y + 2 * PAD, 128), f32),
            pltpu.VMEM((2, X, Y + 2 * PAD, 128), f32),
            pltpu.VMEM((2, X, Y + 2 * PAD, 128), f32),
            pltpu.VMEM((X, 16 + 2 * PAD, 128), f32),
            pltpu.VMEM((X, 16 + 2 * PAD, 128), f32),
            pltpu.VMEM((X, 16 + 2 * PAD, 128), f32),
            pltpu.VMEM((X, 16 + 2 * PAD, 128), f32),
            pltpu.VMEM((X, 8, 128), f32),
            pltpu.VMEM((LEVELS * 24, 128), f32),
            pltpu.VMEM((2, Y, 128), f32),
            pltpu.SemaphoreType.DMA((10,)),
            pltpu.SemaphoreType.DMA((10,)),
            pltpu.SemaphoreType.DMA,
            pltpu.SemaphoreType.DMA((4,)),
            pltpu.SemaphoreType.DMA((4,)),
            pltpu.SemaphoreType.DMA((4,)),
            pltpu.SemaphoreType.DMA((4,)),
        ],
        compiler_params=pltpu.CompilerParams(collective_id=0, has_side_effects=True),
    )(beam_profile, beam_start, beam_steps, layer_heat_coefficients, wafer_state)


def solution(mesh):
    in_specs = (P("scan", "cross", None), P(), P(), P(), P())
    out_specs = P("scan", "cross", None)
    return jax.shard_map(shards, mesh=mesh, in_specs=in_specs, out_specs=out_specs, check_vma=False)
```
